512 devices in a mesh: tm: 128 (over y, z, core), rep: 4 (over x).
Axes of the slice: x: 4, y: 4, z: 16, core: 2. Of those that a mesh axis runs over, the one named last changes fastest.
Arguments:
- separator_inverse: bfloat16 [512, 384, 384], P(('rep', 'tm')), parts along dimension 0, may hold values from -1 to 3, as said below
- separator_lower: bfloat16 [512, 384, 384], P(('rep', 'tm')), parts along dimension 0, may hold values from -0.15625 to 0.15625
- separator_upper: bfloat16 [512, 384, 384], P(('rep', 'tm')), parts along dimension 0, may hold values from -0.15625 to 0.15625
- top_diagonal: bfloat16 [512, 384, 384], P(('rep', 'tm')), parts along dimension 0, may hold values from -1 to 3, as said below
- top_coupling: bfloat16 [512, 384, 384], P(('rep', 'tm')), parts along dimension 0, may hold values from -0.3125 to 0.3125
- interior_inverse: bfloat16 [512, 384, 384], P(('rep', 'tm')), parts along dimension 0, may hold values from -1 to 3, as said below
- interior_lower: bfloat16 [512, 384, 384], P(('rep', 'tm')), parts along dimension 0, may hold values from -0.15625 to 0.15625
- interior_upper: bfloat16 [512, 384, 384], P(('rep', 'tm')), parts along dimension 0, may hold values from -0.15625 to 0.15625
Outputs:
- inverse_diagonal: bfloat16 [1024, 384, 384], P(('rep', 'tm')), parts along dimension 0
- inverse_below: bfloat16 [1024, 384, 384], P(('rep', 'tm')), parts along dimension 0
The draws below stay inside these ranges and needn't reach their ends.
There are 4 independent parts, one for each index of `rep`. The reference program is written for one: setup_inputs(seed, part) draws one part's arguments, and reference() takes and returns one part's arrays. A program takes and returns all parts, laid end to end along the dimension named above; each array names one. Nothing has to cross between parts.
Inputs may be any that keep to these rules, and one draw needn't show every extreme that they name: `separator_inverse`: every block is symmetric. `top_diagonal`: every block is symmetric. `interior_inverse`: every block is symmetric.
All inputs are finite; a program needn't handle non-finite values.
Results may differ from the reference program's by a relative error of at most 0.006.
Values may be sent and summed in bfloat16 or wider, within the bound.
No kernel may reach another device: no remote copies, remote signals or barrier semaphores. Data moves between devices by JAX's collectives and lax.ppermute only.
A program may use at most 64 MiB of HBM per device.

```python
import math
import jax
import jax.numpy as jnp

B = 384
SEPS = 128
LEVELS = 4
TOPGAP = 16


def symmetric_blocks(key):
    diag_key, jitter_key = jax.random.split(key)
    diagonal = jnp.exp(jax.random.uniform(diag_key, (SEPS, B), jnp.float32, math.log(0.5), math.log(2.0)))
    jitter = jnp.clip(jax.random.normal(jitter_key, (SEPS, B, B), jnp.float32), -5.0, 5.0)
    jitter = jitter * (0.6 / math.sqrt(B))
    symmetric = (jitter + jnp.swapaxes(jitter, 1, 2)) * 0.7071
    identity = jnp.eye(B, dtype=jnp.float32)
    return (symmetric + diagonal[:, :, None] * identity[None, :, :]).astype(jnp.bfloat16)


def draw_separator_inverse(key, part):
    return symmetric_blocks(jax.random.fold_in(key, 11))


def draw_top_diagonal(key, part):
    return symmetric_blocks(jax.random.fold_in(key, 23))


def draw_interior_inverse(key, part):
    return symmetric_blocks(jax.random.fold_in(key, 37))


def levels(stream_key, extent, cuts, low, top_value):
    def one(axis_at, blocks):
        draws = jax.random.uniform(jax.random.fold_in(jax.random.fold_in(stream_key, 6), axis_at), (blocks,), jnp.float32, low / len(cuts), top_value / len(cuts))
        return jnp.repeat(jnp.exp(draws), extent[axis_at] // blocks).reshape((-1,) + (1,) * (len(extent) - axis_at - 1))

    gain = one(*cuts[0])
    for cut in cuts[1:]:
        gain = gain * one(*cut)
    return gain


def scatter_about(stream_key, shape, width, limit, cuts=(), kind=jnp.bfloat16):
    values = width * jax.random.normal(stream_key, shape, jnp.float32)
    if cuts:
        values = values * levels(stream_key, shape, cuts, -0.22, 0.18)
    return jnp.clip(values, -limit, limit).astype(kind)


def setup_inputs(seed: int = 0, part: int = 0) -> dict:
    splits = jax.random.split(jax.random.key(seed), 9)
    own_keys = jax.random.split(jax.random.fold_in(splits[8], part), 9)
    separator_inverse = draw_separator_inverse(jax.random.fold_in(jax.random.fold_in(splits[8], part), 71), part)
    separator_lower = scatter_about(own_keys[1], (SEPS, B, B), (4 * B) ** -0.5, 0.15625, ((0, 128),))
    separator_upper = scatter_about(own_keys[2], (SEPS, B, B), (4 * B) ** -0.5, 0.15625, ((0, 128),))
    top_diagonal = draw_top_diagonal(jax.random.fold_in(jax.random.fold_in(splits[8], part), 71), part)
    top_coupling = scatter_about(own_keys[4], (SEPS, B, B), B ** -0.5, 0.3125, ((0, 128),))
    interior_inverse = draw_interior_inverse(jax.random.fold_in(jax.random.fold_in(splits[8], part), 71), part)
    interior_lower = scatter_about(own_keys[6], (SEPS, B, B), (4 * B) ** -0.5, 0.15625, ((0, 128),))
    interior_upper = scatter_about(own_keys[7], (SEPS, B, B), (4 * B) ** -0.5, 0.15625, ((0, 128),))
    return dict(separator_inverse=separator_inverse, separator_lower=separator_lower, separator_upper=separator_upper, top_diagonal=top_diagonal, top_coupling=top_coupling, interior_inverse=interior_inverse, interior_lower=interior_lower, interior_upper=interior_upper)


def product(left_op, right_op):
    return jnp.einsum("nij,njk->nik", left_op.astype(jnp.float32), right_op.astype(jnp.float32))


def product_transposed(left_op, right_op):
    return jnp.einsum("nij,nkj->nik", left_op.astype(jnp.float32), right_op.astype(jnp.float32))


def descend(inverse, lower_mult, upper_mult, lower_diagonal, coupling, upper_diagonal):
    toward_lower = (product(lower_mult, lower_diagonal) + product(upper_mult, coupling)).astype(jnp.bfloat16)
    toward_upper = (product_transposed(lower_mult, coupling) + product(upper_mult, upper_diagonal)).astype(jnp.bfloat16)
    diagonal_new = (inverse.astype(jnp.float32) + product_transposed(toward_lower, lower_mult)
                    + product_transposed(toward_upper, upper_mult)).astype(jnp.bfloat16)
    return toward_lower, toward_upper, diagonal_new


def reference(separator_inverse, separator_lower, separator_upper, top_diagonal, top_coupling,
              interior_inverse, interior_lower, interior_upper):
    margin = TOPGAP // 2

    def rolled(field):
        return jnp.roll(field, margin, axis=0)

    def unrolled(field):
        return jnp.roll(field, -margin, axis=0)

    separator_inverse = rolled(separator_inverse)
    separator_lower = rolled(separator_lower)
    separator_upper = rolled(separator_upper)
    top_diagonal = rolled(top_diagonal)
    top_coupling = rolled(top_coupling)
    interior_inverse = rolled(interior_inverse)
    interior_lower = rolled(interior_lower)
    interior_upper = rolled(interior_upper)
    places = jnp.arange(SEPS)
    blank = jnp.zeros((SEPS, B, B), jnp.bfloat16)
    topmost = (places % TOPGAP == 0)
    sigma_diagonal = jnp.where(topmost[:, None, None], top_diagonal, blank)
    sigma_upper = jnp.where(topmost[:, None, None], top_coupling, blank)
    sigma_lower = blank
    for height in range(LEVELS, 0, -1):
        offset = 2 ** (height - 1)
        stride = 2 * offset
        lower_diagonal = sigma_diagonal[0::stride]
        lower_coupling = sigma_upper[0::stride]
        upper_diagonal = jnp.roll(sigma_diagonal[0::stride], -1, axis=0)
        upper_coupling = jnp.roll(sigma_lower[0::stride], -1, axis=0)
        members = lower_diagonal.shape[0]
        lower_holds = (jnp.arange(members) % 2 == 1) | (height == LEVELS)
        coupling = jnp.where(lower_holds[:, None, None], jnp.swapaxes(lower_coupling, 1, 2), upper_coupling)
        toward_lower, toward_upper, diagonal_new = descend(
            separator_inverse[offset::stride], separator_lower[offset::stride], separator_upper[offset::stride],
            lower_diagonal, coupling, upper_diagonal)
        sigma_lower = sigma_lower.at[offset::stride].set(toward_lower)
        sigma_upper = sigma_upper.at[offset::stride].set(toward_upper)
        sigma_diagonal = sigma_diagonal.at[offset::stride].set(diagonal_new)
    next_diagonal = jnp.roll(sigma_diagonal, -1, axis=0)
    next_lower = jnp.roll(sigma_lower, -1, axis=0)
    odd_slab = (places % 2 == 1)
    coupling = jnp.where(odd_slab[:, None, None], jnp.swapaxes(sigma_upper, 1, 2), next_lower)
    below_own, below_next, interior_diagonal = descend(
        interior_inverse, interior_lower, interior_upper, sigma_diagonal, coupling, next_diagonal)
    sigma_diagonal = unrolled(sigma_diagonal)
    interior_diagonal = unrolled(interior_diagonal)
    below_own = unrolled(below_own)
    below_next = unrolled(below_next)
    inverse_diagonal = jnp.stack([sigma_diagonal, interior_diagonal], axis=1).reshape(2 * SEPS, B, B)
    inverse_below = jnp.stack([below_own, jnp.swapaxes(below_next, 1, 2)], axis=1).reshape(2 * SEPS, B, B)
    return inverse_diagonal, inverse_below
```

```python
import functools

import jax
import jax.numpy as jnp
from jax import lax
from jax.experimental import pallas as pl
from jax.experimental.pallas import tpu as pltpu
from jax.sharding import PartitionSpec as P

BF = jnp.bfloat16
F32 = jnp.float32
NT = (((1,), (1,)), ((), ()))


def mm(left_op, right_op):
    return jnp.dot(left_op, right_op, preferred_element_type=F32)


def mt(left_op, right_op):
    return lax.dot_general(left_op, right_op, NT, preferred_element_type=F32)


def level_kernel(height, holds_all, place, inv, low, up, from_low, from_up, own_up, own_down, out_up, out_down):
    n = low.shape[1]
    stride = 2**height
    removed = lax.rem(place[0], stride) == stride // 2
    holds = jnp.logical_or(holds_all, lax.rem(place[0], 2 * stride) >= stride)

    @pl.when(jnp.logical_not(removed))
    def _():
        out_up[...] = own_up[...]
        out_down[...] = own_down[...]

    def finish():
        diag = inv[0].astype(F32) + mt(out_down[n:, :], low[0]) + mt(out_up[n:, :], up[0])
        diag = diag.astype(BF)
        out_up[:n, :] = diag
        out_down[:n, :] = diag

    @pl.when(jnp.logical_and(removed, holds))
    def _():
        out_down[n:, :] = (mm(low[0], from_low[:n, :]) + mt(up[0], from_low[n:, :])).astype(BF)
        out_up[n:, :] = (mm(low[0], from_low[n:, :]) + mm(up[0], from_up[:n, :])).astype(BF)
        finish()

    @pl.when(jnp.logical_and(removed, jnp.logical_not(holds)))
    def _():
        out_down[n:, :] = (mm(low[0], from_low[:n, :]) + mm(up[0], from_up[n:, :])).astype(BF)
        out_up[n:, :] = (mt(low[0], from_up[n:, :]) + mm(up[0], from_up[:n, :])).astype(BF)
        finish()


def interior_kernel(place, inv, low, up, own_up, next_up, next_down, out_diag, out_below):
    n = low.shape[1]
    out_diag[0] = own_up[:n, :]

    def finish(below, above, next_diag):
        out_below[0] = below.astype(BF)
        above = above.astype(BF)
        out_below[1] = above.T
        diag = inv[0].astype(F32) + mt(out_below[0], low[0]) + mt(above, up[0])
        out_diag[1] = diag.astype(BF)

    @pl.when(lax.rem(place[0], 2) == 1)
    def _():
        finish(
            mm(low[0], own_up[:n, :]) + mt(up[0], own_up[n:, :]),
            mm(low[0], own_up[n:, :]) + mm(up[0], next_up[:n, :]),
            None,
        )

    @pl.when(lax.rem(place[0], 2) == 0)
    def _():
        finish(
            mm(low[0], own_up[:n, :]) + mm(up[0], next_down[n:, :]),
            mt(low[0], next_down[n:, :]) + mm(up[0], next_down[:n, :]),
            None,
        )


def on_device(
    separator_inverse,
    separator_lower,
    separator_upper,
    top_diagonal,
    top_coupling,
    interior_inverse,
    interior_lower,
    interior_upper,
):
    devices = lax.axis_size("tm")
    levels_total = min(4, devices // 4)
    spacing = 2**levels_total
    margin = spacing // 2
    n = separator_lower.shape[1]
    place = ((lax.axis_index("tm") + margin) % devices).astype(jnp.int32).reshape(1)

    def moved(value, places, step):
        pairs = [((p - margin) % devices, (p + step - margin) % devices) for p in places]
        return lax.ppermute(value, "tm", pairs)

    smem = pl.BlockSpec(memory_space=pltpu.SMEM)
    vmem = pl.BlockSpec(memory_space=pltpu.VMEM)
    message = pltpu.VMEM((2 * n, n), BF)

    def near(*values):
        return [pltpu.with_memory_space_constraint(v, pltpu.VMEM) for v in values]


    own_up = jnp.concatenate([top_diagonal[0], top_coupling[0]], axis=0)
    own_down = own_up
    from_up = None
    for height in range(levels_total, 0, -1):
        offset = 2 ** (height - 1)
        stride = 2 * offset
        middles = range(offset, devices, stride)
        from_low = moved(own_up, [m - offset for m in middles], offset)
        from_up = moved(own_down, [m + offset for m in middles], -offset)
        own_up, own_down = pl.pallas_call(
            functools.partial(level_kernel, height, height == levels_total),
            out_shape=(message, message),
            in_specs=[smem] + [vmem] * 7,
            out_specs=(vmem, vmem),
            compiler_params=pltpu.CompilerParams(vmem_limit_bytes=16 << 20),
            name=f"level{height}",
        )(
            place,
            separator_inverse,
            separator_lower,
            separator_upper,
            *near(from_low, from_up, own_up, own_down),
        )
    next_down = moved(own_down, range(1, devices, 2), -1)
    pair = jax.ShapeDtypeStruct((2, n, n), BF)
    return pl.pallas_call(
        interior_kernel,
        out_shape=(pair, pair),
        in_specs=[smem] + [vmem] * 6,
        out_specs=(vmem, vmem),
        compiler_params=pltpu.CompilerParams(vmem_limit_bytes=16 << 20),
        name="interior",
    )(place, interior_inverse, interior_lower, interior_upper, *near(own_up, from_up, next_down))


def solution(mesh):
    spec = P(("rep", "tm"), None, None)
    return jax.shard_map(
        on_device, mesh=mesh, in_specs=(spec,) * 8, out_specs=(spec, spec), check_vma=False
    )
```

```python
import functools

import jax
import jax.numpy as jnp
from jax import lax
from jax.experimental import pallas as pl
from jax.experimental.pallas import tpu as pltpu
from jax.sharding import PartitionSpec as P


BF = jnp.bfloat16
F32 = jnp.float32
NT = (((1,), (1,)), ((), ()))


def mm(left_op, right_op):
    return jnp.dot(left_op, right_op, preferred_element_type=F32)


def mt(left_op, right_op):
    return lax.dot_general(left_op, right_op, NT, preferred_element_type=F32)


def packed_parts(t):
    return (
        ((0, 0), (0, 0), 3 * t),
        ((t, 0), (t, t), 2 * t),
        ((t, 2 * t), (2 * t, 2 * t), t),
    )


def unpack(dst, src, base=0):
    t = dst.shape[0] // 3
    for (pr, pc), (fr, fc), width in packed_parts(t):
        dst[fr : fr + t, fc : fc + width] = src[base + pr : base + pr + t, pc : pc + width]
    dst[t : 2 * t, :t] = src[base : base + t, t : 2 * t].T
    dst[2 * t :, :t] = src[base : base + t, 2 * t :].T
    dst[2 * t :, t : 2 * t] = src[base + t : base + 2 * t, t : 2 * t].T


def eliminate(t, inv, low, up, diag_low, diag_up, coup, coup_holds, out_down, out_up, out_diag):
    if coup_holds:
        down = mm(low, diag_low[...]) + mt(up, coup)
        upw = mm(low, coup) + mm(up, diag_up[...])
    else:
        down = mm(low, diag_low[...]) + mm(up, coup)
        upw = mt(low, coup) + mm(up, diag_up[...])
    down = down.astype(BF)
    upw = upw.astype(BF)
    out_down(down)
    out_up(upw)
    for (pr, pc), (fr, fc), width in packed_parts(t):
        rows = slice(fr, fr + t)
        cols = slice(fc, fc + width)
        part = inv(pr, pc, fr, fc, width).astype(F32)
        part = part + mt(down[rows], low[cols]) + mt(upw[rows], up[cols])
        out_diag(pr, pc, width, part.astype(BF))


def roles(place):
    j = place[0]
    r = lax.rem(j, 16)
    return r, lax.rem(j, 2), lax.div(r, 2)


def pack_kernel(place, inv, low, up, top, coup, up_msg, down_msg, d_msg, in_msg, sems):
    n = low.shape[1]
    t = n // 3
    r, core, chip = roles(place)

    def run(copies):
        for i, (src, dst) in enumerate(copies):
            pltpu.make_async_copy(src, dst, sems.at[i]).start()
        for i, (src, dst) in enumerate(copies):
            pltpu.make_async_copy(src, dst, sems.at[i]).wait()

    def diag_copies(src, dst):
        return [
            (src.at[0, fr : fr + t, fc : fc + width], dst.at[pr : pr + t, pc : pc + width])
            for (pr, pc), (fr, fc), width in packed_parts(t)
        ]

    @pl.when(r == 0)
    def _():
        copies = [(coup.at[0], up_msg.at[2 * t :, :])]
        for dst in (up_msg, d_msg, down_msg):
            copies += diag_copies(top, dst)
        run(copies)

    @pl.when(jnp.logical_or(core == 1, lax.rem(chip, 2) == 1))
    def _():
        copies = diag_copies(inv, in_msg)
        copies.append((low.at[0], in_msg.at[2 * t : 2 * t + n, :]))
        copies.append((up.at[0], in_msg.at[2 * t + n :, :]))
        run(copies)


def level_kernel(height, place, inv, low, up, from_low, from_up, up_in, down_in, d_in,
                 up_msg, down_msg, d_msg, diag_low, diag_up):
    n = low.shape[1]
    t = n // 3
    r, _, _ = roles(place)

    def go(coup, holds):
        unpack(diag_low, from_low)
        unpack(diag_up, from_up)

        def out_down(v):
            down_msg[2 * t :, :] = v

        def out_up(v):
            up_msg[2 * t :, :] = v

        def out_diag(pr, pc, width, v):
            for dst in (up_msg, down_msg, d_msg):
                dst[pr : pr + t, pc : pc + width] = v

        eliminate(
            t, lambda pr, pc, fr, fc, w: inv[0, fr : fr + t, fc : fc + w], low[0], up[0],
            diag_low, diag_up, coup[2 * t :, :], holds, out_down, out_up, out_diag,
        )

    if height == 4:
        @pl.when(r == 8)
        def _():
            go(from_low, True)
    else:
        @pl.when(r == 4)
        def _():
            go(from_up, False)

        @pl.when(r == 12)
        def _():
            go(from_low, True)


def fine_kernel(place, own_in, near_in, first_in, up_msg, d_msg, from_up3, y_two, y_one, y_low, n_low, n_up,
                own, other, lo, hi, mid, half):
    n = up_msg.shape[1]
    t = n // 3
    _, core, chip = roles(place)

    def go(low_src, up_src, coup, holds, second, odd):
        unpack(lo, low_src)
        unpack(hi, up_src)
        mid_packed = other if not odd else own
        mid_row = 2 * t if not odd else 0

        def parts(src):
            return (
                lambda pr, pc, fr, fc, w: src[pr : pr + t, pc : pc + w],
                src[2 * t : 2 * t + n, :],
                src[2 * t + n :, :],
            )

        def keep(v):
            half[...] = v

        def drop(v):
            pass

        def out_mid(pr, pc, width, v):
            mid_packed[mid_row + pr : mid_row + pr + t, pc : pc + width] = v

        eliminate(
            t, *parts(second), lo, hi, coup[2 * t :, :], holds,
            drop if odd else keep, keep if odd else drop, out_mid,
        )
        unpack(mid, mid_packed, mid_row)

        def out_down(v):
            own[4 * t :, :] = v

        def out_up(v):
            other[4 * t :, :] = v

        def out_diag(pr, pc, width, v):
            own[2 * t + pr : 3 * t + pr, pc : pc + width] = v
            other[pr : pr + t, pc : pc + width] = v

        eliminate(
            t, *parts(first_in), mid if odd else lo, hi if odd else mid, half[...], odd,
            out_down, out_up, out_diag,
        )
        if odd:
            other[2 * t : 4 * t, :] = up_src[: 2 * t, :]
        else:
            own[: 2 * t, :] = low_src[: 2 * t, :]

    phase = jnp.where(core == 0, lax.rem(chip, 4), 4)

    @pl.when(phase == 0)
    def _():
        go(d_msg, y_two, y_two, False, near_in, False)

    @pl.when(phase == 1)
    def _():
        go(n_low, y_one, y_one, False, own_in, True)

    @pl.when(phase == 2)
    def _():
        go(up_msg, from_up3, up_msg, True, near_in, False)

    @pl.when(phase == 3)
    def _():
        go(y_low, n_up, y_low, True, own_in, True)


def interior_kernel(place, inv, low, up, own, other, out_diag, out_below, here, above):
    n = low.shape[1]
    t = n // 3
    _, core, _ = roles(place)

    def go(src, holds):
        unpack(here, src)
        unpack(above, src, 2 * t)
        coup = src[4 * t :, :]
        out_diag[0] = here[...]
        if holds:
            p = mm(low[0], here[...]) + mt(up[0], coup)
            q = mm(low[0], coup) + mm(up[0], above[...])
        else:
            p = mm(low[0], here[...]) + mm(up[0], coup)
            q = mt(low[0], coup) + mm(up[0], above[...])
        p = p.astype(BF)
        q = q.astype(BF)
        out_below[0] = p
        out_below[1] = q.T
        out_diag[1] = (inv[0].astype(F32) + mt(p, low[0]) + mt(q, up[0])).astype(BF)

    @pl.when(core == 0)
    def _():
        go(own, False)

    @pl.when(core == 1)
    def _():
        go(other, True)


def on_device(
    separator_inverse,
    separator_lower,
    separator_upper,
    top_diagonal,
    top_coupling,
    interior_inverse,
    interior_lower,
    interior_upper,
):
    devices = lax.axis_size("tm")
    spacing = 16
    margin = spacing // 2
    n = separator_lower.shape[1]
    t = n // 3
    place = lax.rem(lax.axis_index("tm") + margin, devices).astype(jnp.int32).reshape(1)

    def moved(value, select, step):
        pairs = [
            ((p - margin) % devices, (p + step - margin) % devices)
            for p in range(devices)
            if select(p % spacing)
        ]
        return lax.ppermute(value, "tm", pairs)

    smem = pl.BlockSpec(memory_space=pltpu.SMEM)
    vmem = pl.BlockSpec(memory_space=pltpu.VMEM)
    anywhere = pl.BlockSpec(memory_space=pl.ANY)
    params = pltpu.CompilerParams(vmem_limit_bytes=16 << 20)
    block = pltpu.VMEM((n, n), BF)
    message = pltpu.VMEM((2 * t + n, n), BF)
    diagonal = pltpu.VMEM((2 * t, n), BF)
    inputs = pltpu.VMEM((2 * t + 2 * n, n), BF)
    both = pltpu.VMEM((4 * t + n, n), BF)

    def near(*values):
        return [pltpu.with_memory_space_constraint(v, pltpu.VMEM) for v in values]

    up_msg, down_msg, d_msg, in_msg = pl.pallas_call(
        pack_kernel,
        out_shape=(message, message, diagonal, inputs),
        in_specs=[smem] + [anywhere] * 5,
        out_specs=(vmem,) * 4,
        scratch_shapes=[pltpu.SemaphoreType.DMA((10,))],
        compiler_params=params,
        name="pack",
    )(
        place,
        *[
            pltpu.with_memory_space_constraint(v, pltpu.HBM)
            for v in (separator_inverse, separator_lower, separator_upper, top_diagonal, top_coupling)
        ],
    )

    def level(height, from_low, from_up, up_msg, down_msg, d_msg):
        return pl.pallas_call(
            functools.partial(level_kernel, height),
            out_shape=(message, message, diagonal),
            in_specs=[smem] + [vmem] * 8,
            out_specs=(vmem,) * 3,
            scratch_shapes=[block, block],
            input_output_aliases={6: 0, 7: 1, 8: 2},
            compiler_params=params,
        )(
            place,
            separator_inverse,
            separator_lower,
            separator_upper,
            *near(from_low, from_up, up_msg, down_msg, d_msg),
        )

    from_low = moved(up_msg, lambda r: r == 0, 8)
    from_up = moved(d_msg, lambda r: r == 0, -8)
    near_in = moved(in_msg, lambda r: r % 4 == 2, -2)
    first_in = moved(in_msg, lambda r: r % 2 == 1, -1)
    up_msg, down_msg, d_msg = level(4, from_low, from_up, up_msg, down_msg, d_msg)
    from_low = moved(up_msg, lambda r: r % 8 == 0, 4)
    from_up = moved(down_msg, lambda r: r % 8 == 0, -4)
    up_msg, down_msg, d_msg = level(3, from_low, from_up, up_msg, down_msg, d_msg)
    y_two = moved(down_msg, lambda r: r % 8 == 4, -4)
    y_one = moved(down_msg, lambda r: r % 8 == 4, -2)
    y_low = moved(up_msg, lambda r: r % 8 == 4, 2)
    n_low = moved(d_msg, lambda r: r % 8 == 0, 2)
    n_up = moved(d_msg, lambda r: r % 8 == 0, -2)
    own, other = pl.pallas_call(
        fine_kernel,
        out_shape=(both, both),
        in_specs=[smem] + [vmem] * 11,
        out_specs=(vmem,) * 2,
        scratch_shapes=[block] * 4,
        compiler_params=params,
        name="fine",
    )(place, *near(in_msg, near_in, first_in, up_msg, d_msg, from_up, y_two, y_one, y_low, n_low, n_up))
    other = moved(other, lambda r: r % 2 == 0, 1)
    pair = jax.ShapeDtypeStruct((2, n, n), BF)
    return pl.pallas_call(
        interior_kernel,
        out_shape=(pair, pair),
        in_specs=[smem] + [vmem] * 5,
        out_specs=(vmem,) * 2,
        scratch_shapes=[block] * 2,
        compiler_params=params,
        name="interior",
    )(place, interior_inverse, interior_lower, interior_upper, *near(own, other))


def solution(mesh):
    spec = P(("rep", "tm"), None, None)

    return jax.shard_map(
        on_device, mesh=mesh, in_specs=(spec,) * 8, out_specs=(spec, spec), check_vma=False
    )
```

```python
import jax
import jax.numpy as jnp
from jax import lax
from jax.experimental import pallas as pl
from jax.experimental.pallas import tpu as pltpu
from jax.sharding import PartitionSpec as P


BF = jnp.bfloat16
F32 = jnp.float32
NT = (((1,), (1,)), ((), ()))


def mm(left_op, right_op):
    return jnp.dot(left_op, right_op, preferred_element_type=F32)


def mt(left_op, right_op):
    return lax.dot_general(left_op, right_op, NT, preferred_element_type=F32)


def packed_parts(t):
    return (
        ((0, 0), (0, 0), 3 * t),
        ((t, 0), (t, t), 2 * t),
        ((t, 2 * t), (2 * t, 2 * t), t),
    )


def unpack(dst, src, base=0):
    t = dst.shape[0] // 3
    for (pr, pc), (fr, fc), width in packed_parts(t):
        dst[fr : fr + t, fc : fc + width] = src[base + pr : base + pr + t, pc : pc + width]
    dst[t : 2 * t, :t] = src[base : base + t, t : 2 * t].T
    dst[2 * t :, :t] = src[base : base + t, 2 * t :].T
    dst[2 * t :, t : 2 * t] = src[base + t : base + 2 * t, t : 2 * t].T


def eliminate(t, inv, low, up, diag_low, diag_up, coup, coup_holds, out_down, out_up, out_diag):
    if coup_holds:
        down = mm(low, diag_low[...]) + mt(up, coup)
        upw = mm(low, coup) + mm(up, diag_up[...])
    else:
        down = mm(low, diag_low[...]) + mm(up, coup)
        upw = mt(low, coup) + mm(up, diag_up[...])
    down = down.astype(BF)
    upw = upw.astype(BF)
    out_down(down)
    out_up(upw)
    for (pr, pc), (fr, fc), width in packed_parts(t):
        rows = slice(fr, fr + t)
        cols = slice(fc, fc + width)
        part = inv(pr, pc, fr, fc, width).astype(F32)
        part = part + mt(down[rows], low[cols]) + mt(upw[rows], up[cols])
        out_diag(pr, pc, width, part.astype(BF))


def roles(place):
    j = place[0]
    r = lax.rem(j, 16)
    return r, lax.rem(j, 2), lax.div(r, 2)


def pack_kernel(place, inv, low, up, top, coup, up_msg, d_msg, in_msg, sems):
    n = low.shape[1]
    t = n // 3
    r, core, chip = roles(place)

    def run(copies):
        for i, (src, dst) in enumerate(copies):
            pltpu.make_async_copy(src, dst, sems.at[i]).start()
        for i, (src, dst) in enumerate(copies):
            pltpu.make_async_copy(src, dst, sems.at[i]).wait()

    def diag_copies(src, dst):
        return [
            (src.at[0, fr : fr + t, fc : fc + width], dst.at[pr : pr + t, pc : pc + width])
            for (pr, pc), (fr, fc), width in packed_parts(t)
        ]

    @pl.when(r == 0)
    def _():
        copies = [(coup.at[0], up_msg.at[2 * t :, :])]
        for dst in (up_msg, d_msg):
            copies += diag_copies(top, dst)
        run(copies)

    @pl.when(jnp.logical_or(jnp.logical_or(core == 1, lax.rem(chip, 2) == 1), r == 8))
    def _():
        copies = diag_copies(inv, in_msg)
        copies.append((low.at[0], in_msg.at[2 * t : 2 * t + n, :]))
        copies.append((up.at[0], in_msg.at[2 * t + n :, :]))
        run(copies)


def source_parts(t, n, src):
    return (
        lambda pr, pc, fr, fc, w: src[pr : pr + t, pc : pc + w],
        src[2 * t : 2 * t + n, :],
        src[2 * t + n :, :],
    )


def block_parts(t, inv, low, up):
    return (lambda pr, pc, fr, fc, w: inv[0, fr : fr + t, fc : fc + w], low[0], up[0])


def coarse_kernel(place, inv, low, up, early_r, late_r, early_l, late_l, early_in, late_in,
                  up_msg, down_msg, far, lo, hi, mid, half):
    n = low.shape[1]
    t = n // 3

    def go(low_src, up_src, upper_in, upper_half):
        unpack(lo, low_src)
        unpack(hi, up_src)
        mid_packed = far if not upper_half else down_msg

        def keep(v):
            half[...] = v

        def drop(v):
            pass

        def out_mid(pr, pc, width, v):
            mid_packed[pr : pr + t, pc : pc + width] = v

        eliminate(
            t, *source_parts(t, n, upper_in), lo, hi, low_src[2 * t :, :], True,
            drop if upper_half else keep, keep if upper_half else drop, out_mid,
        )
        unpack(mid, mid_packed)

        def out_down(v):
            down_msg[2 * t :, :] = v

        def out_up(v):
            up_msg[2 * t :, :] = v

        def out_diag(pr, pc, width, v):
            up_msg[pr : pr + t, pc : pc + width] = v
            down_msg[pr : pr + t, pc : pc + width] = v

        eliminate(
            t, *block_parts(t, inv, low, up), mid if upper_half else lo, hi if upper_half else mid,
            half[...], upper_half, out_down, out_up, out_diag,
        )
        if upper_half:
            far[...] = up_src[...]

    row = lax.rem(place[0], 32)

    @pl.when(row == 20)
    def _():
        go(early_r, early_l, early_in, False)

    @pl.when(row == 4)
    def _():
        go(late_r, late_l, late_in, False)

    @pl.when(row == 12)
    def _():
        go(early_r, early_l, early_in, True)

    @pl.when(row == 28)
    def _():
        go(late_r, late_l, late_in, True)


def middle_kernel(place, inv, low, up, four_r, four_l, d_in, d_msg, lo, hi):
    n = low.shape[1]
    t = n // 3
    r, _, _ = roles(place)

    @pl.when(r == 8)
    def _():
        unpack(lo, four_r)
        unpack(hi, four_l)

        def drop(v):
            pass

        def out_diag(pr, pc, width, v):
            d_msg[pr : pr + t, pc : pc + width] = v

        eliminate(
            t, *block_parts(t, inv, low, up), lo, hi, four_r[2 * t :, :], True, drop, drop, out_diag
        )


def fine_kernel(place, own_in, near_a, near_b, first_in, up_msg, d_msg, far, y_two, y_one, y_low, n_low, n_up,
                own, other, lo, hi, mid, half):
    n = up_msg.shape[1]
    t = n // 3
    r, core, chip = roles(place)

    def go(low_src, up_src, coup, holds, second, odd):
        unpack(lo, low_src)
        unpack(hi, up_src)
        mid_packed = other if not odd else own
        mid_row = 2 * t if not odd else 0

        def keep(v):
            half[...] = v

        def drop(v):
            pass

        def out_mid(pr, pc, width, v):
            mid_packed[mid_row + pr : mid_row + pr + t, pc : pc + width] = v

        eliminate(
            t, *source_parts(t, n, second), lo, hi, coup[2 * t :, :], holds,
            drop if odd else keep, keep if odd else drop, out_mid,
        )
        unpack(mid, mid_packed, mid_row)

        def out_down(v):
            own[4 * t :, :] = v

        def out_up(v):
            other[4 * t :, :] = v

        def out_diag(pr, pc, width, v):
            own[2 * t + pr : 3 * t + pr, pc : pc + width] = v
            other[pr : pr + t, pc : pc + width] = v

        eliminate(
            t, *source_parts(t, n, first_in), mid if odd else lo, hi if odd else mid, half[...], odd,
            out_down, out_up, out_diag,
        )
        if odd:
            other[2 * t : 4 * t, :] = up_src[: 2 * t, :]
        else:
            own[: 2 * t, :] = low_src[: 2 * t, :]

    phase = jnp.where(core == 0, lax.rem(chip, 4), 4)

    @pl.when(phase == 0)
    def _():
        go(d_msg, y_two, y_two, False, near_a, False)

    @pl.when(phase == 1)
    def _():
        go(n_low, y_one, y_one, False, own_in, True)

    @pl.when(jnp.logical_and(phase == 2, r == 4))
    def _():
        go(up_msg, far, up_msg, True, near_b, False)

    @pl.when(jnp.logical_and(phase == 2, r == 12))
    def _():
        go(up_msg, far, up_msg, True, near_a, False)

    @pl.when(phase == 3)
    def _():
        go(y_low, n_up, y_low, True, own_in, True)


def interior_kernel(place, inv, low, up, own, other, out_diag, out_below, here, above):
    n = low.shape[1]
    t = n // 3
    _, core, _ = roles(place)

    def go(src, holds):
        unpack(here, src)
        unpack(above, src, 2 * t)
        coup = src[4 * t :, :]
        out_diag[0] = here[...]
        if holds:
            p = mm(low[0], here[...]) + mt(up[0], coup)
            q = mm(low[0], coup) + mm(up[0], above[...])
        else:
            p = mm(low[0], here[...]) + mm(up[0], coup)
            q = mt(low[0], coup) + mm(up[0], above[...])
        p = p.astype(BF)
        q = q.astype(BF)
        out_below[0] = p
        out_below[1] = q.T
        out_diag[1] = (inv[0].astype(F32) + mt(p, low[0]) + mt(q, up[0])).astype(BF)

    @pl.when(core == 0)
    def _():
        go(own, False)

    @pl.when(core == 1)
    def _():
        go(other, True)


def on_device(
    separator_inverse,
    separator_lower,
    separator_upper,
    top_diagonal,
    top_coupling,
    interior_inverse,
    interior_lower,
    interior_upper,
):
    devices = lax.axis_size("tm")
    spacing = 16
    margin = spacing // 2
    n = separator_lower.shape[1]
    t = n // 3
    place = lax.rem(lax.axis_index("tm") + margin, devices).astype(jnp.int32).reshape(1)

    def moved(value, *moves):
        pairs = [
            ((p - margin) % devices, (p + step - margin) % devices)
            for p in range(devices)
            for mod, at, step in moves
            if p % mod == at
        ]
        return lax.ppermute(value, "tm", pairs)

    smem = pl.BlockSpec(memory_space=pltpu.SMEM)
    vmem = pl.BlockSpec(memory_space=pltpu.VMEM)
    anywhere = pl.BlockSpec(memory_space=pl.ANY)
    params = pltpu.CompilerParams(vmem_limit_bytes=16 << 20)
    block = pltpu.VMEM((n, n), BF)
    message = pltpu.VMEM((2 * t + n, n), BF)
    diagonal = pltpu.VMEM((2 * t, n), BF)
    inputs = pltpu.VMEM((2 * t + 2 * n, n), BF)
    both = pltpu.VMEM((4 * t + n, n), BF)

    def near(*values):
        return [pltpu.with_memory_space_constraint(v, pltpu.VMEM) for v in values]

    up_msg, d_msg, in_msg = pl.pallas_call(
        pack_kernel,
        out_shape=(message, diagonal, inputs),
        in_specs=[smem] + [anywhere] * 5,
        out_specs=(vmem,) * 3,
        scratch_shapes=[pltpu.SemaphoreType.DMA((7,))],
        compiler_params=params,
        name="pack",
    )(
        place,
        *[
            pltpu.with_memory_space_constraint(v, pltpu.HBM)
            for v in (separator_inverse, separator_lower, separator_upper, top_diagonal, top_coupling)
        ],
    )
    late_in = moved(in_msg, (32, 24, 4), (32, 8, -4))
    early_r = moved(up_msg, (32, 0, 12), (32, 16, 4))
    late_r = moved(up_msg, (32, 16, 12), (32, 0, 4))
    late_l = moved(d_msg, (32, 16, -12), (32, 0, -4))
    early_in = moved(in_msg, (32, 24, -4), (32, 8, 4))
    early_l = moved(d_msg, (32, 0, -12), (32, 16, -4))
    near_a = moved(in_msg, (16, 2, -2), (16, 10, -2), (16, 14, -2))
    near_b = moved(in_msg, (16, 6, -2))
    first_in = moved(in_msg, (2, 1, -1))
    four_r = moved(up_msg, (16, 0, 8))
    four_l = moved(d_msg, (16, 0, -8))
    separators = (separator_inverse, separator_lower, separator_upper)
    up_three, down_msg, far = pl.pallas_call(
        coarse_kernel,
        out_shape=(message, message, diagonal),
        in_specs=[smem] + [vmem] * 9,
        out_specs=(vmem,) * 3,
        scratch_shapes=[block] * 4,
        compiler_params=params,
        name="coarse",
    )(place, *separators, *near(early_r, late_r, early_l, late_l, early_in, late_in))
    y_two = moved(down_msg, (8, 4, -4))
    y_one = moved(down_msg, (8, 4, -2))
    y_low = moved(up_three, (8, 4, 2))
    d_msg = pl.pallas_call(
        middle_kernel,
        out_shape=diagonal,
        in_specs=[smem] + [vmem] * 6,
        out_specs=vmem,
        scratch_shapes=[block] * 2,
        input_output_aliases={6: 0},
        compiler_params=params,
        name="middle",
    )(place, *separators, *near(four_r, four_l, d_msg))
    n_low = moved(d_msg, (8, 0, 2))
    n_up = moved(d_msg, (8, 0, -2))
    own, other = pl.pallas_call(
        fine_kernel,
        out_shape=(both, both),
        in_specs=[smem] + [vmem] * 12,
        out_specs=(vmem,) * 2,
        scratch_shapes=[block] * 4,
        compiler_params=params,
        name="fine",
    )(place, *near(in_msg, near_a, near_b, first_in, up_three, d_msg, far, y_two, y_one, y_low, n_low, n_up))
    other = moved(other, (2, 0, 1))
    pair = jax.ShapeDtypeStruct((2, n, n), BF)
    return pl.pallas_call(
        interior_kernel,
        out_shape=(pair, pair),
        in_specs=[smem] + [vmem] * 5,
        out_specs=(vmem,) * 2,
        scratch_shapes=[block] * 2,
        compiler_params=params,
        name="interior",
    )(place, interior_inverse, interior_lower, interior_upper, *near(own, other))


def solution(mesh):
    spec = P(("rep", "tm"), None, None)

    return jax.shard_map(
        on_device, mesh=mesh, in_specs=(spec,) * 8, out_specs=(spec, spec), check_vma=False
    )
```

```python
import jax
import jax.numpy as jnp
from jax import lax
from jax.experimental import pallas as pl
from jax.experimental.pallas import tpu as pltpu
from jax.sharding import PartitionSpec as P


BF = jnp.bfloat16
F32 = jnp.float32
NT = (((1,), (1,)), ((), ()))


def mm(left_op, right_op):
    return jnp.dot(left_op, right_op, preferred_element_type=F32)


def mt(left_op, right_op):
    return lax.dot_general(left_op, right_op, NT, preferred_element_type=F32)


def packed_parts(t):
    return (
        ((0, 0), (0, 0), 3 * t),
        ((t, 0), (t, t), 2 * t),
        ((t, 2 * t), (2 * t, 2 * t), t),
    )


def unpack(dst, src, base=0):
    t = dst.shape[0] // 3
    for (pr, pc), (fr, fc), width in packed_parts(t):
        dst[fr : fr + t, fc : fc + width] = src[base + pr : base + pr + t, pc : pc + width]
    dst[t : 2 * t, :t] = src[base : base + t, t : 2 * t].T
    dst[2 * t :, :t] = src[base : base + t, 2 * t :].T
    dst[2 * t :, t : 2 * t] = src[base + t : base + 2 * t, t : 2 * t].T


def eliminate(t, inv, low, up, diag_low, diag_up, coup, coup_holds, out_down, out_up, out_diag):
    if coup_holds:
        down = mm(low, diag_low[...]) + mt(up, coup)
        upw = mm(low, coup) + mm(up, diag_up[...])
    else:
        down = mm(low, diag_low[...]) + mm(up, coup)
        upw = mt(low, coup) + mm(up, diag_up[...])
    down = down.astype(BF)
    upw = upw.astype(BF)
    out_down(down)
    out_up(upw)
    for (pr, pc), (fr, fc), width in packed_parts(t):
        rows = slice(fr, fr + t)
        cols = slice(fc, fc + width)
        part = inv(pr, pc, fr, fc, width).astype(F32)
        part = part + mt(down[rows], low[cols]) + mt(upw[rows], up[cols])
        out_diag(pr, pc, width, part.astype(BF))


def roles(place):
    j = place[0]
    r = lax.rem(j, 16)
    return r, lax.rem(j, 2), lax.div(r, 2)


def pack_kernel(place, inv, low, up, top, coup, up_msg, d_msg, in_msg, sems):
    n = low.shape[1]
    t = n // 3
    r, core, chip = roles(place)

    def run(copies):
        for i, (src, dst) in enumerate(copies):
            pltpu.make_async_copy(src, dst, sems.at[i]).start()
        for i, (src, dst) in enumerate(copies):
            pltpu.make_async_copy(src, dst, sems.at[i]).wait()

    def diag_copies(src, dst):
        return [
            (src.at[0, fr : fr + t, fc : fc + width], dst.at[pr : pr + t, pc : pc + width])
            for (pr, pc), (fr, fc), width in packed_parts(t)
        ]

    @pl.when(r == 0)
    def _():
        copies = [(coup.at[0], up_msg.at[2 * t :, :])]
        for dst in (up_msg, d_msg):
            copies += diag_copies(top, dst)
        run(copies)

    @pl.when(jnp.logical_or(jnp.logical_or(core == 1, lax.rem(chip, 2) == 1), r == 8))
    def _():
        copies = diag_copies(inv, in_msg)
        copies.append((low.at[0], in_msg.at[2 * t : 2 * t + n, :]))
        copies.append((up.at[0], in_msg.at[2 * t + n :, :]))
        run(copies)


def source_parts(t, n, src):
    return (
        lambda pr, pc, fr, fc, w: src[pr : pr + t, pc : pc + w],
        src[2 * t : 2 * t + n, :],
        src[2 * t + n :, :],
    )


def block_parts(t, inv, low, up):
    return (lambda pr, pc, fr, fc, w: inv[0, fr : fr + t, fc : fc + w], low[0], up[0])


def coarse_kernel(place, inv, low, up, early_r, late_r, early_l, late_l, early_in, late_in,
                  up_msg, down_msg, far, lo, hi, mid, half):
    n = low.shape[1]
    t = n // 3

    def go(low_src, up_src, upper_in, upper_half):
        unpack(lo, low_src)
        unpack(hi, up_src)
        mid_packed = far if not upper_half else down_msg

        def keep(v):
            half[...] = v

        def drop(v):
            pass

        def out_mid(pr, pc, width, v):
            mid_packed[pr : pr + t, pc : pc + width] = v

        eliminate(
            t, *source_parts(t, n, upper_in), lo, hi, low_src[2 * t :, :], True,
            drop if upper_half else keep, keep if upper_half else drop, out_mid,
        )
        unpack(mid, mid_packed)

        def out_down(v):
            down_msg[2 * t :, :] = v

        def out_up(v):
            up_msg[2 * t :, :] = v

        def out_diag(pr, pc, width, v):
            up_msg[pr : pr + t, pc : pc + width] = v
            down_msg[pr : pr + t, pc : pc + width] = v

        eliminate(
            t, *block_parts(t, inv, low, up), mid if upper_half else lo, hi if upper_half else mid,
            half[...], upper_half, out_down, out_up, out_diag,
        )
        if upper_half:
            far[...] = up_src[...]

    row = lax.rem(place[0], 32)

    @pl.when(row == 20)
    def _():
        go(early_r, early_l, early_in, False)

    @pl.when(row == 4)
    def _():
        go(late_r, late_l, late_in, False)

    @pl.when(row == 12)
    def _():
        go(early_r, early_l, early_in, True)

    @pl.when(row == 28)
    def _():
        go(late_r, late_l, late_in, True)


def middle_kernel(place, inv, low, up, four_r, four_l, d_in, d_msg, lo, hi):
    n = low.shape[1]
    t = n // 3
    r, _, _ = roles(place)

    @pl.when(r == 8)
    def _():
        unpack(lo, four_r)
        unpack(hi, four_l)

        def drop(v):
            pass

        def out_diag(pr, pc, width, v):
            d_msg[pr : pr + t, pc : pc + width] = v

        eliminate(
            t, *block_parts(t, inv, low, up), lo, hi, four_r[2 * t :, :], True, drop, drop, out_diag
        )


def fine_steps(t, n, first_in, own, other, lo, hi, mid, half):
    def go(low_src, up_src, coup, holds, second, odd):
        unpack(lo, low_src)
        unpack(hi, up_src)
        mid_packed = other if not odd else own
        mid_row = 2 * t if not odd else 0

        def keep(v):
            half[...] = v

        def drop(v):
            pass

        def out_mid(pr, pc, width, v):
            mid_packed[mid_row + pr : mid_row + pr + t, pc : pc + width] = v

        eliminate(
            t, *source_parts(t, n, second), lo, hi, coup[2 * t :, :], holds,
            drop if odd else keep, keep if odd else drop, out_mid,
        )
        unpack(mid, mid_packed, mid_row)

        def out_down(v):
            own[4 * t :, :] = v

        def out_up(v):
            other[4 * t :, :] = v

        def out_diag(pr, pc, width, v):
            own[2 * t + pr : 3 * t + pr, pc : pc + width] = v
            other[pr : pr + t, pc : pc + width] = v

        eliminate(
            t, *source_parts(t, n, first_in), mid if odd else lo, hi if odd else mid, half[...], odd,
            out_down, out_up, out_diag,
        )
        if odd:
            other[2 * t : 4 * t, :] = up_src[: 2 * t, :]
        else:
            own[: 2 * t, :] = low_src[: 2 * t, :]

    return go


def even_kernel(place, near_a, near_b, first_in, up_msg, d_msg, far, y_two, own, other, lo, hi, mid, half):
    n = up_msg.shape[1]
    t = n // 3
    r, _, _ = roles(place)
    go = fine_steps(t, n, first_in, own, other, lo, hi, mid, half)

    @pl.when(jnp.logical_or(r == 0, r == 8))
    def _():
        go(d_msg, y_two, y_two, False, near_a, False)

    @pl.when(r == 4)
    def _():
        go(up_msg, far, up_msg, True, near_b, False)

    @pl.when(r == 12)
    def _():
        go(up_msg, far, up_msg, True, near_a, False)


def odd_kernel(place, own_in, first_in, y_one, y_low, n_low, n_up, own_0, other_0, own, other, lo, hi, mid, half):
    n = own_in.shape[1]
    t = n // 3
    r, _, _ = roles(place)
    go = fine_steps(t, n, first_in, own, other, lo, hi, mid, half)

    @pl.when(jnp.logical_or(r == 2, r == 10))
    def _():
        go(n_low, y_one, y_one, False, own_in, True)

    @pl.when(jnp.logical_or(r == 6, r == 14))
    def _():
        go(y_low, n_up, y_low, True, own_in, True)


def interior_kernel(place, inv, low, up, own, other, out_diag, out_below, here, above, p_buf, q_buf, d_buf, sems):
    n = low.shape[1]
    t = n // 3
    _, core, _ = roles(place)
    writes = [
        pltpu.make_async_copy(here, out_diag.at[0], sems.at[0]),
        pltpu.make_async_copy(p_buf, out_below.at[0], sems.at[1]),
        pltpu.make_async_copy(q_buf, out_below.at[1], sems.at[2]),
        pltpu.make_async_copy(d_buf, out_diag.at[1], sems.at[3]),
    ]

    def go(src, holds):
        unpack(here, src)
        writes[0].start()
        unpack(above, src, 2 * t)
        coup = src[4 * t :, :]
        if holds:
            p = mm(low[0], here[...]) + mt(up[0], coup)
            q = mm(low[0], coup) + mm(up[0], above[...])
        else:
            p = mm(low[0], here[...]) + mm(up[0], coup)
            q = mt(low[0], coup) + mm(up[0], above[...])
        p = p.astype(BF)
        q = q.astype(BF)
        p_buf[...] = p
        writes[1].start()
        q_buf[...] = q.T
        writes[2].start()
        d_buf[...] = (inv[0].astype(F32) + mt(p, low[0]) + mt(q, up[0])).astype(BF)
        writes[3].start()

    @pl.when(core == 0)
    def _():
        go(own, False)

    @pl.when(core == 1)
    def _():
        go(other, True)

    for write in writes:
        write.wait()


def on_device(
    separator_inverse,
    separator_lower,
    separator_upper,
    top_diagonal,
    top_coupling,
    interior_inverse,
    interior_lower,
    interior_upper,
):
    devices = lax.axis_size("tm")
    spacing = 16
    margin = spacing // 2
    n = separator_lower.shape[1]
    t = n // 3
    place = lax.rem(lax.axis_index("tm") + margin, devices).astype(jnp.int32).reshape(1)

    def moved(value, *moves):
        pairs = [
            ((p - margin) % devices, (p + step - margin) % devices)
            for p in range(devices)
            for mod, at, step in moves
            if p % mod == at
        ]
        return lax.ppermute(value, "tm", pairs)

    smem = pl.BlockSpec(memory_space=pltpu.SMEM)
    vmem = pl.BlockSpec(memory_space=pltpu.VMEM)
    anywhere = pl.BlockSpec(memory_space=pl.ANY)
    params = pltpu.CompilerParams(vmem_limit_bytes=16 << 20)
    block = pltpu.VMEM((n, n), BF)
    message = pltpu.VMEM((2 * t + n, n), BF)
    diagonal = pltpu.VMEM((2 * t, n), BF)
    inputs = pltpu.VMEM((2 * t + 2 * n, n), BF)
    both = pltpu.VMEM((4 * t + n, n), BF)

    def near(*values):
        return [pltpu.with_memory_space_constraint(v, pltpu.VMEM) for v in values]

    up_msg, d_msg, in_msg = pl.pallas_call(
        pack_kernel,
        out_shape=(message, diagonal, inputs),
        in_specs=[smem] + [anywhere] * 5,
        out_specs=(vmem,) * 3,
        scratch_shapes=[pltpu.SemaphoreType.DMA((7,))],
        compiler_params=params,
        name="pack",
    )(
        place,
        *[
            pltpu.with_memory_space_constraint(v, pltpu.HBM)
            for v in (separator_inverse, separator_lower, separator_upper, top_diagonal, top_coupling)
        ],
    )
    late_in = moved(in_msg, (32, 24, 4), (32, 8, -4))
    early_r = moved(up_msg, (32, 0, 12), (32, 16, 4))
    late_r = moved(up_msg, (32, 16, 12), (32, 0, 4))
    late_l = moved(d_msg, (32, 16, -12), (32, 0, -4))
    early_in = moved(in_msg, (32, 24, -4), (32, 8, 4))
    early_l = moved(d_msg, (32, 0, -12), (32, 16, -4))
    near_a = moved(in_msg, (16, 2, -2), (16, 10, -2), (16, 14, -2))
    near_b = moved(in_msg, (16, 6, -2))
    first_in = moved(in_msg, (2, 1, -1))
    four_r = moved(up_msg, (16, 0, 8))
    four_l = moved(d_msg, (16, 0, -8))
    separators = (separator_inverse, separator_lower, separator_upper)
    up_three, down_msg, far = pl.pallas_call(
        coarse_kernel,
        out_shape=(message, message, diagonal),
        in_specs=[smem] + [vmem] * 9,
        out_specs=(vmem,) * 3,
        scratch_shapes=[block] * 4,
        compiler_params=params,
        name="coarse",
    )(place, *separators, *near(early_r, late_r, early_l, late_l, early_in, late_in))
    y_two = moved(down_msg, (8, 4, -4))
    y_one = moved(down_msg, (8, 4, -2))
    y_low = moved(up_three, (8, 4, 2))
    d_msg = pl.pallas_call(
        middle_kernel,
        out_shape=diagonal,
        in_specs=[smem] + [vmem] * 6,
        out_specs=vmem,
        scratch_shapes=[block] * 2,
        input_output_aliases={6: 0},
        compiler_params=params,
        name="middle",
    )(place, *separators, *near(four_r, four_l, d_msg))
    n_low = moved(d_msg, (8, 0, 2))
    n_up = moved(d_msg, (8, 0, -2))
    own, other = pl.pallas_call(
        even_kernel,
        out_shape=(both, both),
        in_specs=[smem] + [vmem] * 7,
        out_specs=(vmem,) * 2,
        scratch_shapes=[block] * 4,
        compiler_params=params,
        name="even",
    )(place, *near(near_a, near_b, first_in, up_three, d_msg, far, y_two))
    own, other = pl.pallas_call(
        odd_kernel,
        out_shape=(both, both),
        in_specs=[smem] + [vmem] * 8,
        out_specs=(vmem,) * 2,
        scratch_shapes=[block] * 4,
        input_output_aliases={7: 0, 8: 1},
        compiler_params=params,
        name="odd",
    )(place, *near(in_msg, first_in, y_one, y_low, n_low, n_up, own, other))
    other = moved(other, (2, 0, 1))
    pair = jax.ShapeDtypeStruct((2, n, n), BF)
    return pl.pallas_call(
        interior_kernel,
        out_shape=(pair, pair),
        in_specs=[smem] + [vmem] * 5,
        out_specs=(anywhere,) * 2,
        scratch_shapes=[block] * 5 + [pltpu.SemaphoreType.DMA((4,))],
        compiler_params=params,
        name="interior",
    )(place, interior_inverse, interior_lower, interior_upper, *near(own, other))


def solution(mesh):
    spec = P(("rep", "tm"), None, None)

    return jax.shard_map(
        on_device, mesh=mesh, in_specs=(spec,) * 8, out_specs=(spec, spec), check_vma=False
    )
```

```python
import jax
import jax.numpy as jnp
from jax import lax
from jax.experimental import pallas as pl
from jax.experimental.pallas import tpu as pltpu
from jax.sharding import PartitionSpec as P


BF = jnp.bfloat16
F32 = jnp.float32
NT = (((1,), (1,)), ((), ()))


def mm(left_op, right_op):
    return jnp.dot(left_op, right_op, preferred_element_type=F32)


def mt(left_op, right_op):
    return lax.dot_general(left_op, right_op, NT, preferred_element_type=F32)


def packed_parts(t):
    return (
        ((0, 0), (0, 0), 3 * t),
        ((t, 0), (t, t), 2 * t),
        ((t, 2 * t), (2 * t, 2 * t), t),
    )


def unpack(dst, src, base=0):
    t = dst.shape[0] // 3
    for (pr, pc), (fr, fc), width in packed_parts(t):
        dst[fr : fr + t, fc : fc + width] = src[base + pr : base + pr + t, pc : pc + width]
    dst[t : 2 * t, :t] = src[base : base + t, t : 2 * t].T
    dst[2 * t :, :t] = src[base : base + t, 2 * t :].T
    dst[2 * t :, t : 2 * t] = src[base + t : base + 2 * t, t : 2 * t].T


def eliminate(t, inv, low, up, diag_low, diag_up, coup, coup_holds, out_down, out_up, out_diag):
    if coup_holds:
        down = mm(low, diag_low[...]) + mt(up, coup)
        upw = mm(low, coup) + mm(up, diag_up[...])
    else:
        down = mm(low, diag_low[...]) + mm(up, coup)
        upw = mt(low, coup) + mm(up, diag_up[...])
    down = down.astype(BF)
    upw = upw.astype(BF)
    out_down(down)
    out_up(upw)
    for (pr, pc), (fr, fc), width in packed_parts(t):
        rows = slice(fr, fr + t)
        cols = slice(fc, fc + width)
        part = inv(pr, pc, fr, fc, width).astype(F32)
        part = part + mt(down[rows], low[cols]) + mt(upw[rows], up[cols])
        out_diag(pr, pc, width, part.astype(BF))


def roles(place):
    j = place[0]
    r = lax.rem(j, 16)
    return r, lax.rem(j, 2), lax.div(r, 2)


def pack_kernel(place, inv, low, up, top, coup, up_msg, d_msg, in_msg, sems):
    n = low.shape[1]
    t = n // 3
    r, core, chip = roles(place)

    def run(copies):
        for i, (src, dst) in enumerate(copies):
            pltpu.make_async_copy(src, dst, sems.at[i]).start()
        for i, (src, dst) in enumerate(copies):
            pltpu.make_async_copy(src, dst, sems.at[i]).wait()

    def diag_copies(src, dst):
        return [
            (src.at[0, fr : fr + t, fc : fc + width], dst.at[pr : pr + t, pc : pc + width])
            for (pr, pc), (fr, fc), width in packed_parts(t)
        ]

    @pl.when(r == 0)
    def _():
        copies = [(coup.at[0], up_msg.at[2 * t :, :])]
        for dst in (up_msg, d_msg):
            copies += diag_copies(top, dst)
        run(copies)

    @pl.when(jnp.logical_or(jnp.logical_or(core == 1, lax.rem(chip, 2) == 1), jnp.logical_or(r == 8, r == 12)))
    def _():
        copies = diag_copies(inv, in_msg)
        copies.append((low.at[0], in_msg.at[2 * t : 2 * t + n, :]))
        copies.append((up.at[0], in_msg.at[2 * t + n :, :]))
        run(copies)


def source_parts(t, n, src):
    return (
        lambda pr, pc, fr, fc, w: src[pr : pr + t, pc : pc + w],
        src[2 * t : 2 * t + n, :],
        src[2 * t + n :, :],
    )


def block_parts(t, inv, low, up):
    return (lambda pr, pc, fr, fc, w: inv[0, fr : fr + t, fc : fc + w], low[0], up[0])


def message_writers(t, n, *messages):
    def out_coup(v):
        messages[0][2 * t : 2 * t + n, :] = v

    def out_diag(pr, pc, width, v):
        for dst in messages:
            dst[pr : pr + t, pc : pc + width] = v

    return out_coup, out_diag


def drop(*_):
    pass


def outer_level(t, n, low_src, up_src, outer, mid_dst, mid_row, ends, keep_up):
    lo, hi, mid, half = ends
    unpack(lo, low_src)
    unpack(hi, up_src)

    def keep(v):
        half[...] = v

    def out_mid(pr, pc, width, v):
        mid_dst[mid_row + pr : mid_row + pr + t, pc : pc + width] = v

    eliminate(
        t, *outer, lo, hi, low_src[2 * t : 2 * t + n, :], True,
        drop if keep_up else keep, keep if keep_up else drop, out_mid,
    )
    unpack(mid, mid_dst, mid_row)


def lower_steps(t, n, low_src, up_src, outer, own, mid_dst, mid_row, down_msg, up_msg, ends):
    lo, _, mid, half = ends
    outer_level(t, n, low_src, up_src, outer, mid_dst, mid_row, ends, False)
    out_down, _ = message_writers(t, n, down_msg)
    out_up, _ = message_writers(t, n, up_msg)
    _, out_diag = message_writers(t, n, up_msg, down_msg)
    eliminate(t, *own, lo, mid, half[...], False, out_down, out_up, out_diag)


def upper_steps(t, n, low_src, up_src, outer, own, mid_dst, mid_row, down_msg, up_msg, ends):
    _, hi, mid, half = ends
    outer_level(t, n, low_src, up_src, outer, mid_dst, mid_row, ends, True)
    out_down, _ = message_writers(t, n, down_msg)
    if up_msg is None:
        out_up = drop
        _, out_diag = message_writers(t, n, down_msg)
    else:
        out_up, _ = message_writers(t, n, up_msg)
        _, out_diag = message_writers(t, n, up_msg, down_msg)
    eliminate(t, *own, mid, hi, half[...], True, out_down, out_up, out_diag)


def coarse_kernel(place, inv, low, up, early_r, late_r, early_l, late_l, early_in, late_in,
                  up_msg, down_msg, wide, lo, hi, mid, half):
    n = low.shape[1]
    t = n // 3

    def go(low_src, up_src, upper_in, upper_half):
        own = block_parts(t, inv, low, up)
        outer = source_parts(t, n, upper_in)
        ends = (lo, hi, mid, half)
        if upper_half:
            upper_steps(t, n, low_src, up_src, outer, own, wide, 2 * t + n, wide, up_msg, ends)
            up_msg[2 * t + n :, :] = up_src[: 2 * t, :]
        else:
            lower_steps(t, n, low_src, up_src, outer, own, up_msg, 2 * t + n, down_msg, up_msg, ends)

    row = lax.rem(place[0], 32)

    @pl.when(row == 20)
    def _():
        go(early_r, early_l, early_in, False)

    @pl.when(row == 4)
    def _():
        go(late_r, late_l, late_in, False)

    @pl.when(row == 12)
    def _():
        go(early_r, early_l, early_in, True)

    @pl.when(row == 28)
    def _():
        go(late_r, late_l, late_in, True)


def middle_kernel(place, inv, low, up, four_r, four_l, upper_e, upper_l, d_in, d_msg, above, lo, hi, mid, half):
    n = low.shape[1]
    t = n // 3

    def go(upper_in):
        upper_steps(
            t, n, four_r, four_l, block_parts(t, inv, low, up), source_parts(t, n, upper_in),
            d_msg, 0, above, None, (lo, hi, mid, half),
        )

    @pl.when(lax.rem(place[0], 32) == 8)
    def _():
        go(upper_e)

    @pl.when(lax.rem(place[0], 32) == 24)
    def _():
        go(upper_l)


def fine_steps(t, n, first_in, own, other, lo, hi, mid, half):
    def go(low_src, up_src, coup, holds, second, odd, low_row=0, up_row=0):
        unpack(lo, low_src, low_row)
        unpack(hi, up_src, up_row)
        mid_packed = other if not odd else own
        mid_row = 2 * t if not odd else 0

        def keep(v):
            half[...] = v

        def drop(v):
            pass

        def out_mid(pr, pc, width, v):
            mid_packed[mid_row + pr : mid_row + pr + t, pc : pc + width] = v

        eliminate(
            t, *source_parts(t, n, second), lo, hi, coup[2 * t : 2 * t + n, :], holds,
            drop if odd else keep, keep if odd else drop, out_mid,
        )
        unpack(mid, mid_packed, mid_row)

        def out_down(v):
            own[4 * t :, :] = v

        def out_up(v):
            other[4 * t :, :] = v

        def out_diag(pr, pc, width, v):
            own[2 * t + pr : 3 * t + pr, pc : pc + width] = v
            other[pr : pr + t, pc : pc + width] = v

        eliminate(
            t, *source_parts(t, n, first_in), mid if odd else lo, hi if odd else mid, half[...], odd,
            out_down, out_up, out_diag,
        )
        if odd:
            other[2 * t : 4 * t, :] = up_src[up_row : up_row + 2 * t, :]
        else:
            own[: 2 * t, :] = low_src[: 2 * t, :]

    return go


def even_kernel(place, near_a, near_b, first_in, up_msg, d_msg, y_two, above, own, other, lo, hi, mid, half):
    n = up_msg.shape[1]
    t = n // 3
    r, _, _ = roles(place)
    go = fine_steps(t, n, first_in, own, other, lo, hi, mid, half)

    @pl.when(r == 0)
    def _():
        go(d_msg, y_two, y_two, False, near_a, False)

    @pl.when(r == 8)
    def _():
        go(d_msg, above, above, False, near_a, False)

    @pl.when(jnp.logical_or(r == 4, r == 12))
    def _():
        go(up_msg, up_msg, up_msg, True, near_b, False, 0, 2 * t + n)


def odd_kernel(place, own_in, first_in, y_one, y_up, y_low, n_low, own_0, other_0, own, other, lo, hi, mid, half):
    n = own_in.shape[1]
    t = n // 3
    r, _, _ = roles(place)
    go = fine_steps(t, n, first_in, own, other, lo, hi, mid, half)

    @pl.when(r == 2)
    def _():
        go(n_low, y_one, y_one, False, own_in, True)

    @pl.when(r == 10)
    def _():
        go(y_up, y_up, y_up, False, own_in, True, 2 * t + n, 0)

    @pl.when(jnp.logical_or(r == 6, r == 14))
    def _():
        go(y_low, y_low, y_low, True, own_in, True, 0, 2 * t + n)


def interior_kernel(place, inv, low, up, own, other, out_diag, out_below, here, above, p_buf, q_buf, d_buf, sems):
    n = low.shape[1]
    t = n // 3
    _, core, _ = roles(place)
    writes = [
        pltpu.make_async_copy(here, out_diag.at[0], sems.at[0]),
        pltpu.make_async_copy(p_buf, out_below.at[0], sems.at[1]),
        pltpu.make_async_copy(q_buf, out_below.at[1], sems.at[2]),
        pltpu.make_async_copy(d_buf, out_diag.at[1], sems.at[3]),
    ]

    def go(src, holds):
        unpack(here, src)
        writes[0].start()
        unpack(above, src, 2 * t)
        coup = src[4 * t :, :]
        if holds:
            p = mm(low[0], here[...]) + mt(up[0], coup)
            q = mm(low[0], coup) + mm(up[0], above[...])
        else:
            p = mm(low[0], here[...]) + mm(up[0], coup)
            q = mt(low[0], coup) + mm(up[0], above[...])
        p = p.astype(BF)
        q = q.astype(BF)
        p_buf[...] = p
        writes[1].start()
        q_buf[...] = q.T
        writes[2].start()
        d_buf[...] = (inv[0].astype(F32) + mt(p, low[0]) + mt(q, up[0])).astype(BF)
        writes[3].start()

    @pl.when(core == 0)
    def _():
        go(own, False)

    @pl.when(core == 1)
    def _():
        go(other, True)

    for write in writes:
        write.wait()


def on_device(
    separator_inverse,
    separator_lower,
    separator_upper,
    top_diagonal,
    top_coupling,
    interior_inverse,
    interior_lower,
    interior_upper,
):
    devices = lax.axis_size("tm")
    spacing = 16
    margin = spacing // 2
    n = separator_lower.shape[1]
    t = n // 3
    place = lax.rem(lax.axis_index("tm") + margin, devices).astype(jnp.int32).reshape(1)

    def moved(value, *moves):
        pairs = [
            ((p - margin) % devices, (p + step - margin) % devices)
            for p in range(devices)
            for mod, at, step in moves
            if p % mod == at
        ]
        return lax.ppermute(value, "tm", pairs)

    smem = pl.BlockSpec(memory_space=pltpu.SMEM)
    vmem = pl.BlockSpec(memory_space=pltpu.VMEM)
    anywhere = pl.BlockSpec(memory_space=pl.ANY)
    params = pltpu.CompilerParams(vmem_limit_bytes=16 << 20)
    block = pltpu.VMEM((n, n), BF)
    message = pltpu.VMEM((2 * t + n, n), BF)
    diagonal = pltpu.VMEM((2 * t, n), BF)
    inputs = pltpu.VMEM((2 * t + 2 * n, n), BF)
    both = pltpu.VMEM((4 * t + n, n), BF)

    def near(*values):
        return [pltpu.with_memory_space_constraint(v, pltpu.VMEM) for v in values]

    up_msg, d_msg, in_msg = pl.pallas_call(
        pack_kernel,
        out_shape=(message, diagonal, inputs),
        in_specs=[smem] + [anywhere] * 5,
        out_specs=(vmem,) * 3,
        scratch_shapes=[pltpu.SemaphoreType.DMA((7,))],
        compiler_params=params,
        name="pack",
    )(
        place,
        *[
            pltpu.with_memory_space_constraint(v, pltpu.HBM)
            for v in (separator_inverse, separator_lower, separator_upper, top_diagonal, top_coupling)
        ],
    )
    late_in = moved(in_msg, (32, 24, 4), (32, 8, -4))
    early_r = moved(up_msg, (32, 0, 12), (32, 16, 4))
    late_r = moved(up_msg, (32, 16, 12), (32, 0, 4))
    late_l = moved(d_msg, (32, 16, -12), (32, 0, -4))
    early_in = moved(in_msg, (32, 24, -4), (32, 8, 4))
    early_l = moved(d_msg, (32, 0, -12), (32, 16, -4))
    near_a = moved(in_msg, (8, 2, -2))
    near_b = moved(in_msg, (8, 6, -2))
    first_in = moved(in_msg, (2, 1, -1))
    four_r = moved(up_msg, (16, 0, 8))
    four_l = moved(d_msg, (16, 0, -8))
    n_low = moved(d_msg, (16, 0, 2))
    separators = (separator_inverse, separator_lower, separator_upper)
    upper_e = moved(in_msg, (32, 12, -4))
    upper_l = moved(in_msg, (32, 28, -4))
    up_three, down_msg, wide = pl.pallas_call(
        coarse_kernel,
        out_shape=(both, message, both),
        in_specs=[smem] + [vmem] * 9,
        out_specs=(vmem,) * 3,
        scratch_shapes=[block] * 4,
        compiler_params=params,
        name="coarse",
    )(place, *separators, *near(early_r, late_r, early_l, late_l, early_in, late_in))
    y_two = moved(down_msg, (16, 4, -4))
    y_up = moved(wide, (16, 12, -2))
    y_one = moved(down_msg, (16, 4, -2))
    y_low = moved(up_three, (8, 4, 2))
    d_msg, above = pl.pallas_call(
        middle_kernel,
        out_shape=(diagonal, message),
        in_specs=[smem] + [vmem] * 8,
        out_specs=(vmem,) * 2,
        scratch_shapes=[block] * 4,
        input_output_aliases={8: 0},
        compiler_params=params,
        name="middle",
    )(place, *separators, *near(four_r, four_l, upper_e, upper_l, d_msg))
    own, other = pl.pallas_call(
        even_kernel,
        out_shape=(both, both),
        in_specs=[smem] + [vmem] * 7,
        out_specs=(vmem,) * 2,
        scratch_shapes=[block] * 4,
        compiler_params=params,
        name="even",
    )(place, *near(near_a, near_b, first_in, up_three, d_msg, y_two, above))
    own, other = pl.pallas_call(
        odd_kernel,
        out_shape=(both, both),
        in_specs=[smem] + [vmem] * 8,
        out_specs=(vmem,) * 2,
        scratch_shapes=[block] * 4,
        input_output_aliases={7: 0, 8: 1},
        compiler_params=params,
        name="odd",
    )(place, *near(in_msg, first_in, y_one, y_up, y_low, n_low, own, other))
    other = moved(other, (2, 0, 1))
    pair = jax.ShapeDtypeStruct((2, n, n), BF)
    return pl.pallas_call(
        interior_kernel,
        out_shape=(pair, pair),
        in_specs=[smem] + [vmem] * 5,
        out_specs=(anywhere,) * 2,
        scratch_shapes=[block] * 5 + [pltpu.SemaphoreType.DMA((4,))],
        compiler_params=params,
        name="interior",
    )(place, interior_inverse, interior_lower, interior_upper, *near(own, other))


def solution(mesh):
    spec = P(("rep", "tm"), None, None)

    return jax.shard_map(
        on_device, mesh=mesh, in_specs=(spec,) * 8, out_specs=(spec, spec), check_vma=False
    )
```

```python
import jax
import jax.numpy as jnp
from jax import lax
from jax.experimental import pallas as pl
from jax.experimental.pallas import tpu as pltpu
from jax.sharding import PartitionSpec as P


BF = jnp.bfloat16
F32 = jnp.float32
NT = (((1,), (1,)), ((), ()))


def mm(left_op, right_op):
    return jnp.dot(left_op, right_op, preferred_element_type=F32)


def mt(left_op, right_op):
    return lax.dot_general(left_op, right_op, NT, preferred_element_type=F32)


def packed_parts(t):
    return (
        ((0, 0), (0, 0), 3 * t),
        ((t, 0), (t, t), 2 * t),
        ((t, 2 * t), (2 * t, 2 * t), t),
    )


def unpack(w, src, base=0, at=0):
    t = src.shape[1] // 3
    for (pr, pc), (fr, fc), width in packed_parts(t):
        part = src[base + pr : base + pr + t, pc : pc + width]
        w[at + fr : at + fr + t, at + fc : at + fc + width] = part
    w[at + t : at + 2 * t, at : at + t] = src[base : base + t, t : 2 * t].T
    w[at + 2 * t : at + 3 * t, at : at + t] = src[base : base + t, 2 * t :].T
    w[at + 2 * t : at + 3 * t, at + t : at + 2 * t] = src[base + t : base + 2 * t, t : 2 * t].T


def couple(w, coup, holds):
    n = coup.shape[1]
    if holds:
        w[:n, n:] = coup
        w[n:, :n] = coup.T
    else:
        w[n:, :n] = coup
        w[:n, n:] = coup.T


def eliminate(t, inv, low, up, w, out_down, out_up, out_diag):
    n = 3 * t
    pair = jnp.concatenate([low, up], axis=1)
    both = mm(pair, w[...]).astype(BF)
    out_down(both[:, :n])
    out_up(both[:, n:])
    for (pr, pc), (fr, fc), width in packed_parts(t):
        part = inv(pr, pc, fr, fc, width).astype(F32)
        part = part + mt(both[fr : fr + t], pair[fc : fc + width])
        out_diag(pr, pc, width, part.astype(BF))


def roles(place):
    j = place[0]
    r = lax.rem(j, 16)
    return r, lax.rem(j, 2), lax.div(r, 2)


def pack_kernel(place, inv, low, up, top, coup, up_msg, d_msg, in_msg, sems):
    n = low.shape[1]
    t = n // 3
    r, core, chip = roles(place)

    def run(copies):
        for i, (src, dst) in enumerate(copies):
            pltpu.make_async_copy(src, dst, sems.at[i]).start()
        for i, (src, dst) in enumerate(copies):
            pltpu.make_async_copy(src, dst, sems.at[i]).wait()

    def diag_copies(src, dst):
        return [
            (src.at[0, fr : fr + t, fc : fc + width], dst.at[pr : pr + t, pc : pc + width])
            for (pr, pc), (fr, fc), width in packed_parts(t)
        ]

    @pl.when(r == 0)
    def _():
        copies = [(coup.at[0], up_msg.at[2 * t :, :])]
        for dst in (up_msg, d_msg):
            copies += diag_copies(top, dst)
        run(copies)

    @pl.when(jnp.logical_or(jnp.logical_or(core == 1, lax.rem(chip, 2) == 1), jnp.logical_or(r == 8, lax.rem(place[0], 32) == 12)))
    def _():
        copies = diag_copies(inv, in_msg)
        copies.append((low.at[0], in_msg.at[2 * t : 2 * t + n, :]))
        copies.append((up.at[0], in_msg.at[2 * t + n :, :]))
        run(copies)


def source_parts(t, n, src):
    return (
        lambda pr, pc, fr, fc, w: src[pr : pr + t, pc : pc + w],
        src[2 * t : 2 * t + n, :],
        src[2 * t + n :, :],
    )


def block_parts(t, inv, low, up):
    return (lambda pr, pc, fr, fc, w: inv[0, fr : fr + t, fc : fc + w], low[0], up[0])


def message_writers(t, n, *messages):
    def out_coup(v):
        messages[0][2 * t : 2 * t + n, :] = v

    def out_diag(pr, pc, width, v):
        for dst in messages:
            dst[pr : pr + t, pc : pc + width] = v

    return out_coup, out_diag


def drop(*_):
    pass


def outer_level(t, n, low_src, up_src, outer, mid_dst, mid_row, w, upper):
    unpack(w, low_src)
    unpack(w, up_src, 0, n)
    couple(w, low_src[2 * t : 2 * t + n, :], True)

    def keep(v):
        couple(w, v, upper)

    def out_mid(pr, pc, width, v):
        mid_dst[mid_row + pr : mid_row + pr + t, pc : pc + width] = v

    eliminate(t, *outer, w, drop if upper else keep, keep if upper else drop, out_mid)
    unpack(w, mid_dst, mid_row, 0 if upper else n)


def lower_steps(t, n, low_src, up_src, outer, own, mid_dst, mid_row, down_msg, up_msg, w):
    outer_level(t, n, low_src, up_src, outer, mid_dst, mid_row, w, False)
    out_down, _ = message_writers(t, n, down_msg)
    out_up, _ = message_writers(t, n, up_msg)
    _, out_diag = message_writers(t, n, up_msg, down_msg)
    eliminate(t, *own, w, out_down, out_up, out_diag)


def upper_steps(t, n, low_src, up_src, outer, own, mid_dst, mid_row, down_msg, up_msg, w):
    outer_level(t, n, low_src, up_src, outer, mid_dst, mid_row, w, True)
    out_down, _ = message_writers(t, n, down_msg)
    if up_msg is None:
        out_up = drop
        _, out_diag = message_writers(t, n, down_msg)
    else:
        out_up, _ = message_writers(t, n, up_msg)
        _, out_diag = message_writers(t, n, up_msg, down_msg)
    eliminate(t, *own, w, out_down, out_up, out_diag)


def coarse_kernel(place, inv, low, up, early_r, late_r, early_l, late_l, early_in, late_in,
                  near_msg, far_msg, w):
    n = low.shape[1]
    t = n // 3

    def go(low_src, up_src, upper_in, upper_half):
        own = block_parts(t, inv, low, up)
        outer = source_parts(t, n, upper_in)
        if upper_half:
            upper_steps(t, n, low_src, up_src, outer, own, far_msg, 2 * t + n, far_msg, near_msg, w)
        else:
            lower_steps(t, n, low_src, up_src, outer, own, far_msg, 2 * t + n, near_msg, far_msg, w)

    row = lax.rem(place[0], 32)

    @pl.when(row == 20)
    def _():
        go(early_r, early_l, early_in, False)

    @pl.when(row == 4)
    def _():
        go(late_r, late_l, late_in, False)

    @pl.when(row == 12)
    def _():
        go(early_r, early_l, early_in, True)

    @pl.when(row == 28)
    def _():
        go(late_r, late_l, late_in, True)


def middle_kernel(place, inv, low, up, four_r, four_l, upper_e, upper_l, d_in, d_msg, above, w):
    n = low.shape[1]
    t = n // 3

    def go(upper_in):
        upper_steps(
            t, n, four_r, four_l, block_parts(t, inv, low, up), source_parts(t, n, upper_in),
            d_msg, 0, above, None, w,
        )

    @pl.when(lax.rem(place[0], 32) == 8)
    def _():
        go(upper_e)

    @pl.when(lax.rem(place[0], 32) == 24)
    def _():
        go(upper_l)


def inputs_kernel(place, inv, low, up, late_msg, sems):
    n = low.shape[1]
    t = n // 3

    @pl.when(lax.rem(place[0], 32) == 28)
    def _():
        copies = [
            (inv.at[0, fr : fr + t, fc : fc + width], late_msg.at[pr : pr + t, pc : pc + width])
            for (pr, pc), (fr, fc), width in packed_parts(t)
        ]
        copies.append((low.at[0], late_msg.at[2 * t : 2 * t + n, :]))
        copies.append((up.at[0], late_msg.at[2 * t + n :, :]))
        for i, (src, dst) in enumerate(copies):
            pltpu.make_async_copy(src, dst, sems.at[i]).start()
        for i, (src, dst) in enumerate(copies):
            pltpu.make_async_copy(src, dst, sems.at[i]).wait()


def fine_steps(t, n, first_in, own, other, w):
    def go(low_src, up_src, coup, holds, second, odd, low_row=0, up_row=0):
        unpack(w, low_src, low_row)
        unpack(w, up_src, up_row, n)
        couple(w, coup[2 * t : 2 * t + n, :], holds)
        mid_packed = other if not odd else own
        mid_row = 2 * t if not odd else 0

        def keep(v):
            couple(w, v, odd)

        def out_mid(pr, pc, width, v):
            mid_packed[mid_row + pr : mid_row + pr + t, pc : pc + width] = v

        outer = source_parts(t, n, second)
        eliminate(t, *outer, w, drop if odd else keep, keep if odd else drop, out_mid)
        unpack(w, mid_packed, mid_row, 0 if odd else n)

        def out_down(v):
            own[4 * t :, :] = v

        def out_up(v):
            other[4 * t :, :] = v

        def out_diag(pr, pc, width, v):
            own[2 * t + pr : 3 * t + pr, pc : pc + width] = v
            other[pr : pr + t, pc : pc + width] = v

        eliminate(t, *source_parts(t, n, first_in), w, out_down, out_up, out_diag)
        if odd:
            other[2 * t : 4 * t, :] = up_src[up_row : up_row + 2 * t, :]
        else:
            own[: 2 * t, :] = low_src[: 2 * t, :]

    return go


def even_kernel(place, near_a, near_u, near_b, first_in, near_msg, far_msg, early_l, late_l, d_msg, y_two, above,
                own, other, w):
    n = near_msg.shape[1]
    t = n // 3
    r, _, _ = roles(place)
    row = lax.rem(place[0], 32)
    go = fine_steps(t, n, first_in, own, other, w)

    @pl.when(r == 0)
    def _():
        go(d_msg, y_two, y_two, False, near_a, False)

    @pl.when(r == 8)
    def _():
        go(d_msg, above, above, False, near_a, False)

    @pl.when(r == 4)
    def _():
        go(far_msg, far_msg, far_msg, True, near_b, False, 0, 2 * t + n)

    @pl.when(row == 12)
    def _():
        go(near_msg, early_l, near_msg, True, near_u, False)

    @pl.when(row == 28)
    def _():
        go(near_msg, late_l, near_msg, True, near_u, False)


def odd_kernel(place, own_in, first_in, y_mid, y_end, n_low, n_up, own_0, other_0, own, other, w):
    n = own_in.shape[1]
    t = n // 3
    r, _, _ = roles(place)
    go = fine_steps(t, n, first_in, own, other, w)

    @pl.when(r == 2)
    def _():
        go(n_low, y_end, y_end, False, own_in, True)

    @pl.when(r == 10)
    def _():
        go(y_mid, y_mid, y_mid, False, own_in, True, 2 * t + n, 0)

    @pl.when(r == 6)
    def _():
        go(y_mid, y_mid, y_mid, True, own_in, True, 0, 2 * t + n)

    @pl.when(r == 14)
    def _():
        go(y_end, n_up, y_end, True, own_in, True)


def interior_kernel(place, inv, low, up, own, other, out_diag, out_below, w, p_buf, q_buf, d_buf, sems):
    n = low.shape[1]
    t = n // 3
    _, core, _ = roles(place)
    writes = [
        pltpu.make_async_copy(w.at[:n, :n], out_diag.at[0], sems.at[0]),
        pltpu.make_async_copy(p_buf, out_below.at[0], sems.at[1]),
        pltpu.make_async_copy(q_buf, out_below.at[1], sems.at[2]),
        pltpu.make_async_copy(d_buf, out_diag.at[1], sems.at[3]),
    ]

    def go(src, holds):
        unpack(w, src)
        writes[0].start()
        unpack(w, src, 2 * t, n)
        couple(w, src[4 * t :, :], holds)
        pair = jnp.concatenate([low[0], up[0]], axis=1)
        both = mm(pair, w[...]).astype(BF)
        p_buf[...] = both[:, :n]
        writes[1].start()
        q_buf[...] = both[:, n:].T
        writes[2].start()
        d_buf[...] = (inv[0].astype(F32) + mt(both, pair)).astype(BF)
        writes[3].start()

    @pl.when(core == 0)
    def _():
        go(own, False)

    @pl.when(core == 1)
    def _():
        go(other, True)

    for write in writes:
        write.wait()


def on_device(
    separator_inverse,
    separator_lower,
    separator_upper,
    top_diagonal,
    top_coupling,
    interior_inverse,
    interior_lower,
    interior_upper,
):
    devices = lax.axis_size("tm")
    spacing = 16
    margin = spacing // 2
    n = separator_lower.shape[1]
    t = n // 3
    place = lax.rem(lax.axis_index("tm") + margin, devices).astype(jnp.int32).reshape(1)

    def moved(value, *moves):
        pairs = [
            ((p - margin) % devices, (p + step - margin) % devices)
            for p in range(devices)
            for mod, at, step in moves
            if p % mod == at
        ]
        return lax.ppermute(value, "tm", pairs)

    smem = pl.BlockSpec(memory_space=pltpu.SMEM)
    vmem = pl.BlockSpec(memory_space=pltpu.VMEM)
    anywhere = pl.BlockSpec(memory_space=pl.ANY)
    params = pltpu.CompilerParams(vmem_limit_bytes=16 << 20)
    block = pltpu.VMEM((n, n), BF)
    square = pltpu.VMEM((2 * n, 2 * n), BF)
    message = pltpu.VMEM((2 * t + n, n), BF)
    diagonal = pltpu.VMEM((2 * t, n), BF)
    inputs = pltpu.VMEM((2 * t + 2 * n, n), BF)
    both = pltpu.VMEM((4 * t + n, n), BF)

    def near(*values):
        return [pltpu.with_memory_space_constraint(v, pltpu.VMEM) for v in values]

    up_msg, d_msg, in_msg = pl.pallas_call(
        pack_kernel,
        out_shape=(message, diagonal, inputs),
        in_specs=[smem] + [anywhere] * 5,
        out_specs=(vmem,) * 3,
        scratch_shapes=[pltpu.SemaphoreType.DMA((7,))],
        compiler_params=params,
        name="pack",
    )(
        place,
        *[
            pltpu.with_memory_space_constraint(v, pltpu.HBM)
            for v in (separator_inverse, separator_lower, separator_upper, top_diagonal, top_coupling)
        ],
    )
    late_in = moved(in_msg, (32, 24, 4), (32, 8, -4))
    early_r = moved(up_msg, (32, 0, 12), (32, 16, 4))
    late_r = moved(up_msg, (32, 16, 12), (32, 0, 4))
    late_l = moved(d_msg, (32, 16, -12), (32, 0, -4))
    early_in = moved(in_msg, (32, 24, -4), (32, 8, 4))
    early_l = moved(d_msg, (32, 0, -12), (32, 16, -4))
    near_a = moved(in_msg, (8, 2, -2))
    near_u = moved(in_msg, (16, 14, -2))
    near_b = moved(in_msg, (16, 6, -2))
    first_in = moved(in_msg, (2, 1, -1))
    four_r = moved(up_msg, (16, 0, 8))
    four_l = moved(d_msg, (16, 0, -8))
    n_low = moved(d_msg, (16, 0, 2))
    separators = (separator_inverse, separator_lower, separator_upper)
    upper_e = moved(in_msg, (32, 12, -4))
    n_up = moved(d_msg, (16, 0, -2))
    late_msg = pl.pallas_call(
        inputs_kernel,
        out_shape=inputs,
        in_specs=[smem] + [anywhere] * 3,
        out_specs=vmem,
        scratch_shapes=[pltpu.SemaphoreType.DMA((5,))],
        compiler_params=params,
        name="inputs",
    )(place, *[pltpu.with_memory_space_constraint(v, pltpu.HBM) for v in separators])
    upper_l = moved(late_msg, (32, 28, -4))
    near_msg, far_msg = pl.pallas_call(
        coarse_kernel,
        out_shape=(message, both),
        in_specs=[smem] + [vmem] * 9,
        out_specs=(vmem,) * 2,
        scratch_shapes=[square],
        compiler_params=params,
        name="coarse",
    )(place, *separators, *near(early_r, late_r, early_l, late_l, early_in, late_in))
    y_two = moved(near_msg, (16, 4, -4))
    y_mid = moved(far_msg, (16, 4, 2), (16, 12, -2))
    y_end = moved(near_msg, (16, 4, -2), (16, 12, 2))
    d_msg, above = pl.pallas_call(
        middle_kernel,
        out_shape=(diagonal, message),
        in_specs=[smem] + [vmem] * 8,
        out_specs=(vmem,) * 2,
        scratch_shapes=[square],
        input_output_aliases={8: 0},
        compiler_params=params,
        name="middle",
    )(place, *separators, *near(four_r, four_l, upper_e, upper_l, d_msg))
    own, other = pl.pallas_call(
        even_kernel,
        out_shape=(both, both),
        in_specs=[smem] + [vmem] * 11,
        out_specs=(vmem,) * 2,
        scratch_shapes=[square],
        compiler_params=params,
        name="even",
    )(place, *near(near_a, near_u, near_b, first_in, near_msg, far_msg, early_l, late_l, d_msg, y_two, above))
    own, other = pl.pallas_call(
        odd_kernel,
        out_shape=(both, both),
        in_specs=[smem] + [vmem] * 8,
        out_specs=(vmem,) * 2,
        scratch_shapes=[square],
        input_output_aliases={7: 0, 8: 1},
        compiler_params=params,
        name="odd",
    )(place, *near(in_msg, first_in, y_mid, y_end, n_low, n_up, own, other))
    other = moved(other, (2, 0, 1))
    pair = jax.ShapeDtypeStruct((2, n, n), BF)
    return pl.pallas_call(
        interior_kernel,
        out_shape=(pair, pair),
        in_specs=[smem] + [vmem] * 5,
        out_specs=(anywhere,) * 2,
        scratch_shapes=[square] + [block] * 3 + [pltpu.SemaphoreType.DMA((4,))],
        compiler_params=params,
        name="interior",
    )(place, interior_inverse, interior_lower, interior_upper, *near(own, other))


def solution(mesh):
    spec = P(("rep", "tm"), None, None)

    return jax.shard_map(
        on_device, mesh=mesh, in_specs=(spec,) * 8, out_specs=(spec, spec), check_vma=False
    )
```

```python
import jax
import jax.numpy as jnp
from jax import lax
from jax.experimental import pallas as pl
from jax.experimental.pallas import tpu as pltpu
from jax.sharding import PartitionSpec as P


BF = jnp.bfloat16
F32 = jnp.float32
NT = (((1,), (1,)), ((), ()))


def mm(left_op, right_op):
    return jnp.dot(left_op, right_op, preferred_element_type=F32)


def mt(left_op, right_op):
    return lax.dot_general(left_op, right_op, NT, preferred_element_type=F32)


def packed_parts(t):
    return (
        ((0, 0), (0, 0), 3 * t),
        ((t, 0), (t, t), 2 * t),
        ((t, 2 * t), (2 * t, 2 * t), t),
    )


def unpack(w, src, base=0, at=0):
    t = src.shape[1] // 3
    for (pr, pc), (fr, fc), width in packed_parts(t):
        part = src[base + pr : base + pr + t, pc : pc + width]
        w[at + fr : at + fr + t, at + fc : at + fc + width] = part
    w[at + t : at + 2 * t, at : at + t] = src[base : base + t, t : 2 * t].T
    w[at + 2 * t : at + 3 * t, at : at + t] = src[base : base + t, 2 * t :].T
    w[at + 2 * t : at + 3 * t, at + t : at + 2 * t] = src[base + t : base + 2 * t, t : 2 * t].T


def couple(w, coup, holds):
    n = coup.shape[1]
    if holds:
        w[:n, n:] = coup
        w[n:, :n] = coup.T
    else:
        w[n:, :n] = coup
        w[:n, n:] = coup.T


def eliminate(t, inv, low, up, w, out_down, out_up, out_diag):
    n = 3 * t
    pair = jnp.concatenate([low, up], axis=1)
    both = mm(pair, w[...]).astype(BF)
    out_down(both[:, :n])
    out_up(both[:, n:])
    for (pr, pc), (fr, fc), width in packed_parts(t):
        part = inv(pr, pc, fr, fc, width).astype(F32)
        part = part + mt(both[fr : fr + t], pair[fc : fc + width])
        out_diag(pr, pc, width, part.astype(BF))


def roles(place):
    j = place[0]
    r = lax.rem(j, 16)
    return r, lax.rem(j, 2), lax.div(r, 2)


def pack_kernel(place, inv, low, up, top, coup, up_msg, d_msg, in_msg, sems):
    n = low.shape[1]
    t = n // 3
    r, core, chip = roles(place)

    def run(copies):
        for i, (src, dst) in enumerate(copies):
            pltpu.make_async_copy(src, dst, sems.at[i]).start()
        for i, (src, dst) in enumerate(copies):
            pltpu.make_async_copy(src, dst, sems.at[i]).wait()

    def diag_copies(src, dst):
        return [
            (src.at[0, fr : fr + t, fc : fc + width], dst.at[pr : pr + t, pc : pc + width])
            for (pr, pc), (fr, fc), width in packed_parts(t)
        ]

    @pl.when(r == 0)
    def _():
        copies = [(coup.at[0], up_msg.at[2 * t :, :])]
        for dst in (up_msg, d_msg):
            copies += diag_copies(top, dst)
        run(copies)

    @pl.when(jnp.logical_or(jnp.logical_or(core == 1, lax.rem(chip, 2) == 1), jnp.logical_or(r == 8, lax.rem(place[0], 32) == 12)))
    def _():
        copies = diag_copies(inv, in_msg)
        copies.append((low.at[0], in_msg.at[2 * t : 2 * t + n, :]))
        copies.append((up.at[0], in_msg.at[2 * t + n :, :]))
        run(copies)


def source_parts(t, n, src):
    return (
        lambda pr, pc, fr, fc, w: src[pr : pr + t, pc : pc + w],
        src[2 * t : 2 * t + n, :],
        src[2 * t + n :, :],
    )


def block_parts(t, inv, low, up):
    return (lambda pr, pc, fr, fc, w: inv[0, fr : fr + t, fc : fc + w], low[0], up[0])


def message_writers(t, n, *messages):
    def out_coup(v):
        messages[0][2 * t : 2 * t + n, :] = v

    def out_diag(pr, pc, width, v):
        for dst in messages:
            dst[pr : pr + t, pc : pc + width] = v

    return out_coup, out_diag


def drop(*_):
    pass


def outer_level(t, n, low_src, up_src, outer, mid_dst, mid_row, w, upper):
    unpack(w, low_src)
    unpack(w, up_src, 0, n)
    couple(w, low_src[2 * t : 2 * t + n, :], True)

    def keep(v):
        couple(w, v, upper)

    def out_mid(pr, pc, width, v):
        mid_dst[mid_row + pr : mid_row + pr + t, pc : pc + width] = v

    eliminate(t, *outer, w, drop if upper else keep, keep if upper else drop, out_mid)
    unpack(w, mid_dst, mid_row, 0 if upper else n)


def lower_steps(t, n, low_src, up_src, outer, own, mid_dst, mid_row, down_msg, up_msg, w):
    outer_level(t, n, low_src, up_src, outer, mid_dst, mid_row, w, False)
    out_down, _ = message_writers(t, n, down_msg)
    out_up, _ = message_writers(t, n, up_msg)
    _, out_diag = message_writers(t, n, up_msg, down_msg)
    eliminate(t, *own, w, out_down, out_up, out_diag)


def upper_steps(t, n, low_src, up_src, outer, own, mid_dst, mid_row, down_msg, up_msg, w):
    outer_level(t, n, low_src, up_src, outer, mid_dst, mid_row, w, True)
    out_down, _ = message_writers(t, n, down_msg)
    if up_msg is None:
        out_up = drop
        _, out_diag = message_writers(t, n, down_msg)
    else:
        out_up, _ = message_writers(t, n, up_msg)
        _, out_diag = message_writers(t, n, up_msg, down_msg)
    eliminate(t, *own, w, out_down, out_up, out_diag)


def coarse_kernel(place, inv, low, up, early_r, late_r, early_l, late_l, early_in, late_in,
                  near_msg, far_msg, w):
    n = low.shape[1]
    t = n // 3

    def go(low_src, up_src, upper_in, upper_half):
        own = block_parts(t, inv, low, up)
        outer = source_parts(t, n, upper_in)
        if upper_half:
            upper_steps(t, n, low_src, up_src, outer, own, far_msg, 2 * t + n, far_msg, near_msg, w)
        else:
            lower_steps(t, n, low_src, up_src, outer, own, far_msg, 2 * t + n, near_msg, far_msg, w)

    row = lax.rem(place[0], 32)

    @pl.when(row == 20)
    def _():
        go(early_r, early_l, early_in, False)

    @pl.when(row == 4)
    def _():
        go(late_r, late_l, late_in, False)

    @pl.when(row == 12)
    def _():
        go(early_r, early_l, early_in, True)

    @pl.when(row == 28)
    def _():
        go(late_r, late_l, late_in, True)


def middle_kernel(place, inv, low, up, four_r, four_l, upper_e, upper_l, d_in, d_msg, above, w):
    n = low.shape[1]
    t = n // 3

    def go(upper_in):
        upper_steps(
            t, n, four_r, four_l, block_parts(t, inv, low, up), source_parts(t, n, upper_in),
            d_msg, 0, above, None, w,
        )

    @pl.when(lax.rem(place[0], 32) == 8)
    def _():
        go(upper_e)

    @pl.when(lax.rem(place[0], 32) == 24)
    def _():
        go(upper_l)


def inputs_kernel(place, inv, low, up, late_msg, sems):
    n = low.shape[1]
    t = n // 3

    @pl.when(lax.rem(place[0], 32) == 28)
    def _():
        copies = [
            (inv.at[0, fr : fr + t, fc : fc + width], late_msg.at[pr : pr + t, pc : pc + width])
            for (pr, pc), (fr, fc), width in packed_parts(t)
        ]
        copies.append((low.at[0], late_msg.at[2 * t : 2 * t + n, :]))
        copies.append((up.at[0], late_msg.at[2 * t + n :, :]))
        for i, (src, dst) in enumerate(copies):
            pltpu.make_async_copy(src, dst, sems.at[i]).start()
        for i, (src, dst) in enumerate(copies):
            pltpu.make_async_copy(src, dst, sems.at[i]).wait()


def fine_steps(t, n, first_in, own, other, w):
    def go(low_src, up_src, coup, holds, second, odd, low_row=0, up_row=0):
        unpack(w, low_src, low_row)
        unpack(w, up_src, up_row, n)
        couple(w, coup[2 * t : 2 * t + n, :], holds)
        mid_packed = other if not odd else own
        mid_row = 2 * t if not odd else 0

        def keep(v):
            couple(w, v, odd)

        def out_mid(pr, pc, width, v):
            mid_packed[mid_row + pr : mid_row + pr + t, pc : pc + width] = v

        outer = source_parts(t, n, second)
        eliminate(t, *outer, w, drop if odd else keep, keep if odd else drop, out_mid)
        unpack(w, mid_packed, mid_row, 0 if odd else n)

        def out_down(v):
            own[4 * t :, :] = v

        def out_up(v):
            other[4 * t :, :] = v

        def out_diag(pr, pc, width, v):
            own[2 * t + pr : 3 * t + pr, pc : pc + width] = v
            other[pr : pr + t, pc : pc + width] = v

        eliminate(t, *source_parts(t, n, first_in), w, out_down, out_up, out_diag)
        if odd:
            other[2 * t : 4 * t, :] = up_src[up_row : up_row + 2 * t, :]
        else:
            own[: 2 * t, :] = low_src[: 2 * t, :]

    return go


def even_kernel(place, near_a, near_u, near_b, first_in, near_msg, far_msg, early_l, late_l, d_msg, y_two, above,
                own, other, w):
    n = near_msg.shape[1]
    t = n // 3
    r, _, _ = roles(place)
    row = lax.rem(place[0], 32)
    go = fine_steps(t, n, first_in, own, other, w)

    @pl.when(r == 0)
    def _():
        go(d_msg, y_two, y_two, False, near_a, False)

    @pl.when(r == 8)
    def _():
        go(d_msg, above, above, False, near_a, False)

    @pl.when(r == 4)
    def _():
        go(far_msg, far_msg, far_msg, True, near_b, False, 0, 2 * t + n)

    @pl.when(row == 12)
    def _():
        go(near_msg, early_l, near_msg, True, near_u, False)

    @pl.when(row == 28)
    def _():
        go(near_msg, late_l, near_msg, True, near_u, False)


def odd_kernel(place, own_in, first_in, y_mid, y_end, n_low, n_up, own_0, other_0, own, other, w):
    n = own_in.shape[1]
    t = n // 3
    r, _, _ = roles(place)
    go = fine_steps(t, n, first_in, own, other, w)

    @pl.when(r == 2)
    def _():
        go(n_low, y_end, y_end, False, own_in, True)

    @pl.when(r == 10)
    def _():
        go(y_mid, y_mid, y_mid, False, own_in, True, 2 * t + n, 0)

    @pl.when(r == 6)
    def _():
        go(y_mid, y_mid, y_mid, True, own_in, True, 0, 2 * t + n)

    @pl.when(r == 14)
    def _():
        go(y_end, n_up, y_end, True, own_in, True)


def interior_kernel(place, inv, low, up, own, other, out_diag, out_below, w, p_buf, q_buf, d_buf, sems):
    n = low.shape[1]
    t = n // 3
    _, core, _ = roles(place)
    writes = [
        pltpu.make_async_copy(w.at[:n, :n], out_diag.at[0], sems.at[0]),
        pltpu.make_async_copy(p_buf, out_below.at[0], sems.at[1]),
        pltpu.make_async_copy(q_buf, out_below.at[1], sems.at[2]),
        pltpu.make_async_copy(d_buf.at[:, : 2 * t], out_diag.at[1, :, : 2 * t], sems.at[3]),
        pltpu.make_async_copy(d_buf.at[:, 2 * t :], out_diag.at[1, :, 2 * t :], sems.at[4]),
    ]

    def go(src, holds):
        unpack(w, src)
        writes[0].start()
        unpack(w, src, 2 * t, n)
        couple(w, src[4 * t :, :], holds)
        pair = jnp.concatenate([low[0], up[0]], axis=1)
        both = mm(pair, w[...]).astype(BF)
        p_buf[...] = both[:, :n]
        writes[1].start()
        q_buf[...] = both[:, n:].T
        writes[2].start()
        d_buf[:, : 2 * t] = (inv[0, :, : 2 * t].astype(F32) + mt(both, pair[: 2 * t])).astype(BF)
        writes[3].start()
        d_buf[:, 2 * t :] = (inv[0, :, 2 * t :].astype(F32) + mt(both, pair[2 * t :])).astype(BF)
        writes[4].start()

    @pl.when(core == 0)
    def _():
        go(own, False)

    @pl.when(core == 1)
    def _():
        go(other, True)

    for write in writes:
        write.wait()


def on_device(
    separator_inverse,
    separator_lower,
    separator_upper,
    top_diagonal,
    top_coupling,
    interior_inverse,
    interior_lower,
    interior_upper,
):
    devices = lax.axis_size("tm")
    spacing = 16
    margin = spacing // 2
    n = separator_lower.shape[1]
    t = n // 3
    place = lax.rem(lax.axis_index("tm") + margin, devices).astype(jnp.int32).reshape(1)

    def moved(value, *moves):
        pairs = [
            ((p - margin) % devices, (p + step - margin) % devices)
            for p in range(devices)
            for mod, at, step in moves
            if p % mod == at
        ]
        return lax.ppermute(value, "tm", pairs)

    smem = pl.BlockSpec(memory_space=pltpu.SMEM)
    vmem = pl.BlockSpec(memory_space=pltpu.VMEM)
    anywhere = pl.BlockSpec(memory_space=pl.ANY)
    params = pltpu.CompilerParams(vmem_limit_bytes=16 << 20)
    block = pltpu.VMEM((n, n), BF)
    square = pltpu.VMEM((2 * n, 2 * n), BF)
    message = pltpu.VMEM((2 * t + n, n), BF)
    diagonal = pltpu.VMEM((2 * t, n), BF)
    inputs = pltpu.VMEM((2 * t + 2 * n, n), BF)
    both = pltpu.VMEM((4 * t + n, n), BF)

    def near(*values):
        return [pltpu.with_memory_space_constraint(v, pltpu.VMEM) for v in values]

    up_msg, d_msg, in_msg = pl.pallas_call(
        pack_kernel,
        out_shape=(message, diagonal, inputs),
        in_specs=[smem] + [anywhere] * 5,
        out_specs=(vmem,) * 3,
        scratch_shapes=[pltpu.SemaphoreType.DMA((7,))],
        compiler_params=params,
        name="pack",
    )(
        place,
        *[
            pltpu.with_memory_space_constraint(v, pltpu.HBM)
            for v in (separator_inverse, separator_lower, separator_upper, top_diagonal, top_coupling)
        ],
    )
    late_in = moved(in_msg, (32, 24, 4), (32, 8, -4))
    early_r = moved(up_msg, (32, 0, 12), (32, 16, 4))
    late_r = moved(up_msg, (32, 16, 12), (32, 0, 4))
    late_l = moved(d_msg, (32, 16, -12), (32, 0, -4))
    early_in = moved(in_msg, (32, 24, -4), (32, 8, 4))
    early_l = moved(d_msg, (32, 0, -12), (32, 16, -4))
    near_a = moved(in_msg, (8, 2, -2))
    near_u = moved(in_msg, (16, 14, -2))
    near_b = moved(in_msg, (16, 6, -2))
    first_in = moved(in_msg, (2, 1, -1))
    four_r = moved(up_msg, (16, 0, 8))
    four_l = moved(d_msg, (16, 0, -8))
    n_low = moved(d_msg, (16, 0, 2))
    separators = (separator_inverse, separator_lower, separator_upper)
    upper_e = moved(in_msg, (32, 12, -4))
    n_up = moved(d_msg, (16, 0, -2))
    late_msg = pl.pallas_call(
        inputs_kernel,
        out_shape=inputs,
        in_specs=[smem] + [anywhere] * 3,
        out_specs=vmem,
        scratch_shapes=[pltpu.SemaphoreType.DMA((5,))],
        compiler_params=params,
        name="inputs",
    )(place, *[pltpu.with_memory_space_constraint(v, pltpu.HBM) for v in separators])
    upper_l = moved(late_msg, (32, 28, -4))
    near_msg, far_msg = pl.pallas_call(
        coarse_kernel,
        out_shape=(message, both),
        in_specs=[smem] + [vmem] * 9,
        out_specs=(vmem,) * 2,
        scratch_shapes=[square],
        compiler_params=params,
        name="coarse",
    )(place, *separators, *near(early_r, late_r, early_l, late_l, early_in, late_in))
    y_two = moved(near_msg, (16, 4, -4))
    y_mid = moved(far_msg, (16, 4, 2), (16, 12, -2))
    y_end = moved(near_msg, (16, 4, -2), (16, 12, 2))
    d_msg, above = pl.pallas_call(
        middle_kernel,
        out_shape=(diagonal, message),
        in_specs=[smem] + [vmem] * 8,
        out_specs=(vmem,) * 2,
        scratch_shapes=[square],
        input_output_aliases={8: 0},
        compiler_params=params,
        name="middle",
    )(place, *separators, *near(four_r, four_l, upper_e, upper_l, d_msg))
    own, other = pl.pallas_call(
        even_kernel,
        out_shape=(both, both),
        in_specs=[smem] + [vmem] * 11,
        out_specs=(vmem,) * 2,
        scratch_shapes=[square],
        compiler_params=params,
        name="even",
    )(place, *near(near_a, near_u, near_b, first_in, near_msg, far_msg, early_l, late_l, d_msg, y_two, above))
    own, other = pl.pallas_call(
        odd_kernel,
        out_shape=(both, both),
        in_specs=[smem] + [vmem] * 8,
        out_specs=(vmem,) * 2,
        scratch_shapes=[square],
        input_output_aliases={7: 0, 8: 1},
        compiler_params=params,
        name="odd",
    )(place, *near(in_msg, first_in, y_mid, y_end, n_low, n_up, own, other))
    other = moved(other, (2, 0, 1))
    pair = jax.ShapeDtypeStruct((2, n, n), BF)
    return pl.pallas_call(
        interior_kernel,
        out_shape=(pair, pair),
        in_specs=[smem] + [vmem] * 5,
        out_specs=(anywhere,) * 2,
        scratch_shapes=[square] + [block] * 3 + [pltpu.SemaphoreType.DMA((5,))],
        compiler_params=params,
        name="interior",
    )(place, interior_inverse, interior_lower, interior_upper, *near(own, other))


def solution(mesh):
    spec = P(("rep", "tm"), None, None)

    return jax.shard_map(
        on_device, mesh=mesh, in_specs=(spec,) * 8, out_specs=(spec, spec), check_vma=False
    )
```
